32 devices in a mesh: we: 4 (over y, x), sn: 8 (over z, core).
Axes of the slice: x: 2, y: 2, z: 4, core: 2. Of those that a mesh axis runs over, the one named last changes fastest.
Arguments:
- velocity: float32 [3, 16, 96, 128], P(None, 'we', 'sn'), may hold values from -6 to 6
- stress: float32 [6, 16, 96, 128], P(None, 'we', 'sn'), may hold values from -6 to 6
- memory: float32 [6, 16, 96, 128], P(None, 'we', 'sn'), may hold values from -3 to 3
- material_code: int32 [16, 96, 128], P('we', 'sn'), may hold values from 0 to 15
- block_scale: float32 [4, 24, 4], P('we', 'sn'), may hold values from 0.5 to 2
- material_table: float32 [6, 16], replicated, may hold values from 0.2 to 3, as said below
- source_cell: int32 [4, 8, 4], P('we', 'sn'), may hold values from 0 to 6143, as said below
- source_amp: float32 [4, 8, 4, 4], P('we', 'sn'), may hold values from -24 to 24
Outputs:
- velocity_out: float32 [3, 16, 96, 128], P(None, 'we', 'sn')
- stress_out: float32 [6, 16, 96, 128], P(None, 'we', 'sn')
- memory_out: float32 [6, 16, 96, 128], P(None, 'we', 'sn')
The draws below stay inside these ranges and needn't reach their ends.
Inputs may be any that keep to these rules, and one draw needn't show every extreme that they name: Rows of material_table lie in: buoyancy 0.6 to 1.4, first Lame parameter 0.5 to 2, shear modulus 0.3 to 1.5, decay 0.5 to 0.98, weight 0.2 to 0.8, cohesion 0.3 to 3. `source_cell`: each entry is c = x 12 * 128 + y * 128 + z for a cell (x, y, z) of the device's own block; cells may repeat.
All inputs are finite; a program needn't handle non-finite values.
Results may differ from the reference program's by a relative error of at most 0.0001.
Values sent between devices are 32-bit elements; how exact they have to be, the bound alone decides.
No kernel may reach another device: no remote copies, remote signals or barrier semaphores. Data moves between devices by JAX's collectives and lax.ppermute only.
A program may use at most 64 MiB of HBM per device.

```python
import math
import jax
import jax.numpy as jnp
from jax import lax

CX = 4
CY = 12
CZ = 128
STEPS = 4
NMAT = 16
BLK = 4
BLKZ = 32
NSRC_DEV = 4
DEV_WE = 4
DEV_SN = 8
NX = 16
NY = 96
NZ = 128


def draw_material_table(key, part):
    uniform_draw = jax.random.uniform(key, (6, NMAT), jnp.float32)
    lower = jnp.array([0.6, 0.5, 0.3, 0.5, 0.2, 0.3], jnp.float32)
    upper = jnp.array([1.4, 2.0, 1.5, 0.98, 0.8, 3.0], jnp.float32)
    return lower[:, None] + (upper - lower)[:, None] * uniform_draw


def draw_source_cell(key, part):
    picks = jax.random.randint(jax.random.fold_in(key, 17), (DEV_WE, DEV_SN, NSRC_DEV), 0, CX * CY * CZ, jnp.int32)
    picks = picks.at[0, 0, 0].set(0)
    return picks.at[DEV_WE - 1, DEV_SN - 1, NSRC_DEV - 1].set(CX * CY * CZ - 1)


def place_ends(entries, rng, smallest, top_value):
    spot = [jax.random.randint(jax.random.fold_in(rng, axis), (), 0, length) for axis, length in enumerate(entries.shape)]
    main_axis = entries.shape.index(max(entries.shape))
    beside = spot[:main_axis] + [(spot[main_axis] + 1) % entries.shape[main_axis]] + spot[main_axis + 1:]
    return entries.at[tuple(spot)].set(smallest).at[tuple(beside)].set(top_value)


def shard_levels(key, extent, split, smallest, top_value):
    def one(dim, parts):
        steps = jax.random.uniform(jax.random.fold_in(jax.random.fold_in(key, 6), dim), (parts,), jnp.float32, smallest / len(split), top_value / len(split))
        return jnp.repeat(jnp.exp(steps), extent[dim] // parts).reshape((-1,) + (1,) * (len(extent) - dim - 1))

    factor_of = one(*split[0])
    for cut in split[1:]:
        factor_of = factor_of * one(*cut)
    return factor_of


def noise(rng, dims, width, bound, shards=(), dtype=jnp.bfloat16):
    entries = jax.random.normal(rng, dims, jnp.float32) * width
    if len(shards) > 0:
        entries = shard_levels(rng, dims, shards, -0.22, 0.18) * entries
    return jnp.clip(entries, min=-bound, max=bound).astype(dtype)


def setup_inputs(seed: int = 0) -> dict:
    arg_keys = jax.random.split(jax.random.key(seed), 9)
    velocity = noise(arg_keys[0], (3, NX, NY, NZ), 1.0, 6.0, ((1, 4), (2, 8)), jnp.float32)
    stress = noise(arg_keys[1], (6, NX, NY, NZ), 1.0, 6.0, ((1, 4), (2, 8)), jnp.float32)
    memory = noise(arg_keys[2], (6, NX, NY, NZ), 0.5, 3.0, ((1, 4), (2, 8)), jnp.float32)
    material_code = place_ends(jax.random.randint(arg_keys[3], (NX, NY, NZ), 0, NMAT), jax.random.fold_in(arg_keys[3], 1), 0, NMAT - 1).astype(jnp.int32)
    block_scale = jnp.clip(jnp.exp(math.log(2.0) - 1.3862944 * jax.random.uniform(arg_keys[4], (NX // BLK, NY // BLK, NZ // BLKZ), jnp.float32) ** shard_levels(arg_keys[4], (NX // BLK, NY // BLK, NZ // BLKZ), ((0, 4), (1, 8)), -0.2, 0.2)), 0.5, 2.0)
    material_table = draw_material_table(jax.random.fold_in(arg_keys[8], 71), 0)
    source_cell = draw_source_cell(jax.random.fold_in(arg_keys[8], 71), 0)
    source_amp = noise(arg_keys[7], (DEV_WE, DEV_SN, NSRC_DEV, STEPS), 4.0, 24.0, ((0, 4), (1, 8)), jnp.float32)
    return {"velocity": velocity, "stress": stress, "memory": memory, "material_code": material_code, "block_scale": block_scale, "material_table": material_table, "source_cell": source_cell, "source_amp": source_amp}


inner_coef = 9.0 / 8.0
outer_coef = 1.0 / 24.0
time_step = 0.08
friction = 0.4

def shifted(padded, along_dim, offset):
    length = padded.shape[along_dim] - 4
    return lax.slice_in_dim(padded, 2 + offset, 2 + offset + length, axis=along_dim)

def forward(padded, along_dim):
    return inner_coef * (shifted(padded, along_dim, 1) - shifted(padded, along_dim, 0)) - outer_coef * (shifted(padded, along_dim, 2) - shifted(padded, along_dim, -1))

def backward(padded, along_dim):
    return inner_coef * (shifted(padded, along_dim, 0) - shifted(padded, along_dim, -1)) - outer_coef * (shifted(padded, along_dim, 1) - shifted(padded, along_dim, -2))

def depth_pad(fields):
    return jnp.pad(fields, ((0, 0), (0, 0), (0, 0), (2, 2)))

def velocity_step(velocity, stress, east_pad, north_pad, buoyancy):
    depth_stress = depth_pad(stress[1::2])
    force_east = forward(east_pad[0], 0) + backward(north_pad[0], 1) + backward(depth_stress[0], 2)
    force_north = backward(east_pad[2], 0) + forward(north_pad[2], 1) + backward(depth_stress[1], 2)
    force_depth = backward(east_pad[1], 0) + backward(north_pad[1], 1) + forward(depth_stress[2], 2)
    return velocity + time_step * buoyancy * jnp.stack([force_east, force_north, force_depth])

def stress_step(stress, memory, east_vel, north_vel, velocity, lame, shear_mod, decay, weight):
    depth_vel = depth_pad(velocity)
    rate_ee = backward(east_vel[0], 0)
    north_east = forward(east_vel[1], 0)
    depth_east = forward(east_vel[2], 0)
    east_north = forward(north_vel[0], 1)
    rate_nn = backward(north_vel[1], 1)
    depth_north = forward(north_vel[2], 1)
    east_depth = forward(depth_vel[0], 2)
    north_depth = forward(depth_vel[1], 2)
    rate_dd = backward(depth_vel[2], 2)
    volume_rate = rate_ee + rate_nn + rate_dd
    rates = jnp.stack([lame * volume_rate + 2.0 * shear_mod * rate_ee, shear_mod * (east_depth + depth_east), shear_mod * (east_north + north_east), shear_mod * (north_depth + depth_north), lame * volume_rate + 2.0 * shear_mod * rate_nn, lame * volume_rate + 2.0 * shear_mod * rate_dd])
    memory_new = decay * memory + (1.0 - decay) * weight * rates
    trial = stress + time_step * (rates - 0.5 * (memory + memory_new))
    return (trial, memory_new)

def plastic(trial, cohesion):
    normal_mask = jnp.array([1.0, 0.0, 0.0, 0.0, 1.0, 1.0], jnp.float32)[:, None, None, None]
    square_weights = jnp.array([0.5, 1.0, 1.0, 1.0, 0.5, 0.5], jnp.float32)[:, None, None, None]
    mean_stress = (trial[0] + trial[4] + trial[5]) / 3.0
    deviator = trial - normal_mask * mean_stress
    second_inv = lax.optimization_barrier(jnp.sum(square_weights * deviator * deviator, 0))
    yield_level = cohesion + friction * jax.nn.softplus(-mean_stress)
    scaled = second_inv / (yield_level * yield_level)
    factor = lax.rsqrt(jnp.sqrt(1.0 + scaled * scaled))
    return normal_mask * mean_stress + factor * deviator

def reference(velocity, stress, memory, material_code, block_scale, material_table, source_cell, source_amp):
    table_rows = material_table[:, material_code]
    scale_full = jnp.repeat(jnp.repeat(jnp.repeat(block_scale, BLK, 0), BLK, 1), BLKZ, 2)
    buoyancy = table_rows[0]
    lame = table_rows[1] * scale_full
    shear_mod = table_rows[2] * scale_full
    decay = table_rows[3]
    weight = table_rows[4]
    cohesion = table_rows[5]
    shape = source_cell.shape
    device_east = lax.broadcasted_iota(jnp.int32, shape, 0)
    device_north = lax.broadcasted_iota(jnp.int32, shape, 1)
    east_cell = device_east * CX + source_cell // (CY * CZ)
    north_cell = device_north * CY + source_cell // CZ % CY
    depth_cell = source_cell % CZ
    source_cells = ((east_cell * NY + north_cell) * NZ + depth_cell).reshape(-1).astype(jnp.int32)
    strengths = source_amp.reshape(-1, STEPS)
    normal_rows = jnp.array([0, 4, 5], jnp.int32)
    for turn_index in range(STEPS):
        east_pad = jnp.pad(stress[0:3], ((0, 0), (2, 2), (0, 0), (0, 0)))
        north_pad = jnp.pad(stress[2:5], ((0, 0), (0, 0), (2, 2), (0, 0)))
        velocity = velocity_step(velocity, stress, east_pad, north_pad, buoyancy)
        east_vel = jnp.pad(velocity, ((0, 0), (2, 2), (0, 0), (0, 0)))
        north_vel = jnp.pad(velocity, ((0, 0), (0, 0), (2, 2), (0, 0)))
        trial, memory = stress_step(stress, memory, east_vel, north_vel, velocity, lame, shear_mod, decay, weight)
        flat = trial.reshape(6, -1)
        flat = flat.at[normal_rows[:, None], source_cells[None, :]].add(time_step * strengths[:, turn_index][None, :])
        trial = flat.reshape(stress.shape)
        stress = plastic(trial, cohesion)
    return (velocity, stress, memory)
```

```python
import functools

import jax
import jax.numpy as jnp
from jax import lax
from jax.experimental import pallas as pl
from jax.experimental.pallas import tpu as pltpu
from jax.sharding import PartitionSpec as P

BLK = 4
BLKZ = 32
LANES = 128
SUB = 8

inner_coef = 9.0 / 8.0
outer_coef = 1.0 / 24.0
ratio = outer_coef / inner_coef
time_step = 0.08
friction = 0.4

VEL, STR, MEM, COD = 0, 3, 9, 15
FIELDS = 16
NORMAL = (0, 4, 5)


def round_up(value, step):
    return -(-value // step) * step


def pack_kernel(vel, stress, mem, code, scale, cell, amp, out, *, cx, cy):
    plane = cy
    field = cx * cy
    for c in range(3):
        for p in range(cx):
            at = (VEL + c) * field + p * plane
            out[at : at + cy, :] = vel[c, p]
    for c in range(6):
        for p in range(cx):
            at = (STR + c) * field + p * plane
            out[at : at + cy, :] = stress[c, p]
            at = (MEM + c) * field + p * plane
            out[at : at + cy, :] = mem[c, p]
    for p in range(cx):
        at = COD * field + p * plane
        out[at : at + cy, :] = (code[p] + 1).astype(jnp.float32)
    tail = FIELDS * field
    lane = lax.broadcasted_iota(jnp.int32, (1, LANES), 1)
    here = tail
    for i in range(scale.shape[0]):
        for j in range(scale.shape[1]):
            row = jnp.zeros((1, LANES), jnp.float32)
            for k in range(scale.shape[2]):
                row = jnp.where(lane // BLKZ == k, scale[i, j, k], row)
            out[here : here + 1, :] = row
            here += 1
    out[here : out.shape[0], :] = jnp.zeros((out.shape[0] - here, LANES), jnp.float32)
    count, steps = amp.shape[2], amp.shape[3]
    row = jnp.zeros((1, LANES), jnp.float32)
    for k in range(count):
        row = jnp.where(lane == k, cell[0, 0, k].astype(jnp.float32), row)
        for t in range(steps):
            row = jnp.where(lane == count + k * steps + t, amp[0, 0, k, t], row)
    out[out.shape[0] - 1 : out.shape[0], :] = row


def step_kernel(*refs, cx, cy, steps, sources, window, dests, fixed):
    count = 3 * len(dests)
    blocks = refs[:count]
    table, place_ref = refs[count : count + 2]
    out_vel, out_str, out_mem = refs[count + 2 : count + 5]
    vel, stress, mem, codes, scales, buoy, lame, shear, decay, weight, cohesion = refs[
        count + 5 : count + 16
    ]
    points, sem = refs[count + 16 :]
    field = cx * cy
    tail = FIELDS * field
    size = blocks[0].shape[0]
    margin = 4
    rows = codes.shape[1]

    me_we = place_ref[0]
    odd = lax.rem(place_ref[1], 2)
    if fixed is None:
        own = me_we * cx
    else:
        own = fixed

    copies = []
    for b in range(count):
        copy = pltpu.make_async_copy(
            blocks[b].at[size - SUB : size, :], points.at[b * SUB : (b + 1) * SUB, :], sem.at[b]
        )
        copy.start()
        copies.append(copy)

    zero = jnp.zeros((rows, LANES), jnp.float32)
    for p in (0, 1, window + 2, window + 3):
        for c in range(3):
            vel[c, p] = zero
            stress[c, p] = zero

    def base_plane(s):
        if fixed is None:
            return jnp.bitwise_xor(me_we, dests[s]) * cx
        return fixed - dests[s] * cx

    def place(block, plane, row):
        def piece(f, p):
            at = f * field + p * cy
            return block[at : at + cy, :]

        for p in range(cx):
            for c in range(3):
                vel[c, plane + p + 2, pl.ds(row, cy), :] = piece(VEL + c, p)
            for c in range(6):
                stress[c, plane + p + 2, pl.ds(row, cy), :] = piece(STR + c, p)
                mem[c, plane + p, pl.ds(row, cy), :] = piece(MEM + c, p)
            codes[plane + p, pl.ds(row, cy), :] = piece(COD, p)
        across = cy // BLK
        for i in range(cx // BLK):
            for j in range(across):
                at = tail + i * across + j
                line = jnp.broadcast_to(block[at : at + 1, :], (BLK, LANES))
                scales[plane // BLK + i, pl.ds(row + j * BLK, BLK), :] = line

    for s in range(len(dests)):
        plane = base_plane(s)
        center, outer, inner = blocks[3 * s : 3 * s + 3]
        place(center, plane, margin + cy)

        @pl.when(odd == 0)
        def _():
            place(outer, plane, margin)
            place(inner, plane, margin + 2 * cy)

        @pl.when(odd == 1)
        def _():
            place(inner, plane, margin)
            place(outer, plane, margin + 2 * cy)

    def properties(p, carry):
        for r in range(0, rows, SUB):
            index = codes[p, r : r + SUB, :].astype(jnp.int32)
            index = jnp.clip(index, 0, LANES - 1)

            def row_of(k):
                line = jnp.broadcast_to(table[k : k + 1, :], (SUB, LANES))
                return jnp.take_along_axis(line, index, axis=1)

            grow = scales[p // BLK, r : r + SUB, :]
            kept = row_of(3)
            buoy[p, r : r + SUB, :] = row_of(0)
            lame[p, r : r + SUB, :] = row_of(1) * grow
            shear[p, r : r + SUB, :] = row_of(2) * grow
            decay[p, r : r + SUB, :] = kept
            weight[p, r : r + SUB, :] = row_of(4)
            cohesion[p, r : r + SUB, :] = row_of(5)
        return carry

    lax.fori_loop(0, window, properties, 0)
    for copy in copies:
        copy.wait()

    lane = lax.broadcasted_iota(jnp.int32, (SUB, LANES), 1)

    def deep(f, k):
        moved = pltpu.roll(f, (-k) % LANES, 1)
        return jnp.where((lane + k >= 0) & (lane + k < LANES), moved, 0.0)

    def z_back(f):
        return f - deep(f, -1), deep(f, 1) - deep(f, -2)

    def z_fore(f):
        return deep(f, 1) - f, deep(f, 2) - deep(f, -1)

    def add(*pairs):
        one, two = pairs[0]
        for a, b in pairs[1:]:
            one = one + a
            two = two + b
        return one - ratio * two

    def reader(ref, c, p, r):
        def at(dp, dr):
            return ref[c, p + 2 + dp, r + dr : r + dr + SUB, :]

        def x_fore():
            return at(1, 0) - at(0, 0), at(2, 0) - at(-1, 0)

        def x_back():
            return at(0, 0) - at(-1, 0), at(1, 0) - at(-2, 0)

        def y_fore():
            return at(0, 1) - at(0, 0), at(0, 2) - at(0, -1)

        def y_back():
            return at(0, 0) - at(0, -1), at(0, 1) - at(0, -2)

        return at, x_fore, x_back, y_fore, y_back

    def tiles(reach):
        need = cy + 2 * reach
        n = -(-need // SUB)
        start = margin + cy - reach
        return [start + SUB * i for i in range(n)]

    def planes(reach):
        need = min(cx + 2 * reach, window)
        if fixed is not None:
            return fixed - reach, cx + 2 * reach
        devices = window // cx
        need = max(
            min(w * cx + cx + reach, window) - max(w * cx - reach, 0) for w in range(devices)
        )
        return jnp.clip(own - reach, 0, window - need), need

    def velocity_phase(reach):
        first, n = planes(reach)

        def body(i, carry):
            p = first + i
            for r in tiles(reach):
                _, xx_fore, _, _, _ = reader(stress, 0, p, r)
                xz, _, xz_back, _, _ = reader(stress, 1, p, r)
                _, _, xy_xback, _, xy_yback = reader(stress, 2, p, r)
                yz, _, _, _, yz_back = reader(stress, 3, p, r)
                _, _, _, yy_fore, _ = reader(stress, 4, p, r)
                zz, _, _, _, _ = reader(stress, 5, p, r)
                push = buoy[p, r : r + SUB, :]
                forces = (
                    add(xx_fore(), xy_yback(), z_back(xz(0, 0))),
                    add(xy_xback(), yy_fore(), z_back(yz(0, 0))),
                    add(xz_back(), yz_back(), z_fore(zz(0, 0))),
                )
                for c in range(3):
                    vel[c, p + 2, r : r + SUB, :] = vel[c, p + 2, r : r + SUB, :] + push * forces[c]
            return carry

        lax.fori_loop(0, n, body, 0)

    def add_sources(t):
        for s in range(len(dests)):
            plane = base_plane(s)
            for which in range(3):
                b = 3 * s + which
                if which == 0:
                    row = margin + cy
                elif which == 1:
                    row = jnp.where(odd == 0, margin, margin + 2 * cy)
                else:
                    row = jnp.where(odd == 0, margin + 2 * cy, margin)
                for k in range(sources):
                    cell = points[b * SUB + SUB - 1, k].astype(jnp.int32)
                    size_plane = cy * LANES
                    p = plane + cell // size_plane
                    r = row + lax.rem(cell, size_plane) // LANES
                    z = lax.rem(cell, LANES)
                    amount = time_step * points[b * SUB + SUB - 1, sources + k * steps + t]
                    line = jnp.where(lane[0:1] == z, amount, 0.0)
                    for c in NORMAL:
                        stress[c, p + 2, pl.ds(r, 1), :] = stress[c, p + 2, pl.ds(r, 1), :] + line

    def stress_phase(reach, last):
        first, n = planes(reach)

        def body(i, carry):
            p = first + i
            for j, r in enumerate(tiles(reach)):
                ve, _, ve_xback, ve_yfore, _ = reader(vel, 0, p, r)
                vn, vn_xfore, _, _, vn_yback = reader(vel, 1, p, r)
                vd, vd_xfore, _, vd_yfore, _ = reader(vel, 2, p, r)
                exx = add(ve_xback())
                eyy = add(vn_yback())
                ezz = add(z_back(vd(0, 0)))
                exz = add(z_fore(ve(0, 0)), vd_xfore())
                exy = add(ve_yfore(), vn_xfore())
                eyz = add(z_fore(vn(0, 0)), vd_yfore())
                mu = shear[p, r : r + SUB, :]
                twice = mu + mu
                bulk = lame[p, r : r + SUB, :] * (exx + eyy + ezz)
                moves = (
                    bulk + twice * exx,
                    mu * exz,
                    mu * exy,
                    mu * eyz,
                    bulk + twice * eyy,
                    bulk + twice * ezz,
                )
                keep = decay[p, r : r + SUB, :]
                gain = weight[p, r : r + SUB, :]
                trial = []
                rest = []
                for c in range(6):
                    old = mem[c, p, r : r + SUB, :]
                    new = keep * old + gain * moves[c]
                    rest.append(new)
                    now = stress[c, p + 2, r : r + SUB, :]
                    trial.append((now + moves[c]) - (0.5 * time_step) * (old + new))
                mean = (trial[0] + trial[4] + trial[5]) * (1.0 / 3.0)
                dxx, dyy, dzz = trial[0] - mean, trial[4] - mean, trial[5] - mean
                dxz, dxy, dyz = trial[1], trial[2], trial[3]
                second = 0.5 * (dxx * dxx + dyy * dyy + dzz * dzz) + (
                    dxz * dxz + dxy * dxy + dyz * dyz
                )
                soft = jnp.maximum(-mean, 0.0) + jnp.log(1.0 + jnp.exp(-jnp.abs(mean)))
                level = cohesion[p, r : r + SUB, :] + friction * soft
                scaled = second / (level * level)
                factor = lax.rsqrt(jnp.sqrt(1.0 + scaled * scaled))
                done = (
                    mean + factor * dxx,
                    factor * dxz,
                    factor * dxy,
                    factor * dyz,
                    mean + factor * dyy,
                    mean + factor * dzz,
                )
                if last:
                    lo = SUB * j
                    n_rows = min(SUB, cy - lo)
                    now_vel = (ve(0, 0), vn(0, 0), vd(0, 0))
                    for c in range(3):
                        out_vel[c, i, lo : lo + n_rows, :] = now_vel[c][:n_rows]
                    for c in range(6):
                        out_str[c, i, lo : lo + n_rows, :] = done[c][:n_rows]
                        out_mem[c, i, lo : lo + n_rows, :] = rest[c][:n_rows]
                else:
                    for c in range(6):
                        stress[c, p + 2, r : r + SUB, :] = done[c]
                        mem[c, p, r : r + SUB, :] = rest[c]
            return carry

        lax.fori_loop(0, n, body, 0)

    for t in range(steps):
        left = 3 * (steps - 1 - t)
        velocity_phase(left + 2)
        add_sources(t)
        stress_phase(left, t == steps - 1)


def shards(
    velocity, stress, memory, material_code, block_scale, material_table, source_cell, source_amp
):
    _, cx, cy, cz = velocity.shape
    sources, steps = source_amp.shape[2:]
    n_we, n_sn = lax.axis_size("we"), lax.axis_size("sn")
    reach = 3 * steps
    assert cz == LANES and cy >= reach and cx % BLK == 0 and cy % BLK == 0
    assert sources * (steps + 1) <= LANES

    used = FIELDS * cx * cy + (cx // BLK) * (cy // BLK) + 1
    vmem = pl.BlockSpec(memory_space=pltpu.VMEM)
    smem = pl.BlockSpec(memory_space=pltpu.SMEM)
    own = pl.pallas_call(
        functools.partial(pack_kernel, cx=cx, cy=cy),
        out_shape=jax.ShapeDtypeStruct((round_up(used, SUB), LANES), jnp.float32),
        in_specs=[vmem, vmem, vmem, vmem, smem, smem, smem],
        out_specs=vmem,
        name="pack",
    )(velocity, stress, memory, material_code, block_scale, source_cell, source_amp)

    width = -(-reach // cx)
    everything = n_we <= 2 * width + 1 and n_we & (n_we - 1) == 0
    if everything:
        dests = list(range(n_we))
        window, fixed = n_we * cx, None
        moves = [[(i, i ^ k) for i in range(n_we)] for k in dests]
    else:
        dests = [0] + [sign * k for k in range(1, width + 1) for sign in (1, -1)]
        window, fixed = (2 * width + 1) * cx, width * cx
        moves = [[(i, i + k) for i in range(n_we) if 0 <= i + k < n_we] for k in dests]
    inner = [(i, i ^ 1) for i in range(n_sn) if i ^ 1 < n_sn]
    outer = [(i, i - 1 + 2 * (i % 2)) for i in range(n_sn)]
    outer = [(a, b) for a, b in outer if 0 <= b < n_sn]
    blocks = []
    for k, move in zip(dests, moves):
        block = own if k == 0 else lax.ppermute(own, "we", move)
        blocks += [block, lax.ppermute(block, "sn", outer), lax.ppermute(block, "sn", inner)]

    decay = material_table[3]
    per_step = time_step * inner_coef
    table = jnp.stack(
        [
            material_table[0] * per_step,
            material_table[1] * per_step,
            material_table[2] * per_step,
            decay,
            (1.0 - decay) * material_table[4] / time_step,
            material_table[5],
        ]
    )
    table = jnp.pad(table, ((0, 2), (1, LANES - 1 - table.shape[1])))

    place = jnp.stack([lax.axis_index("we"), lax.axis_index("sn")])

    margin = 4
    rows = round_up(3 * cy + 2 * margin, SUB) + SUB
    frame = pltpu.VMEM((window, rows, LANES), jnp.float32)

    def frames(n, extra):
        return pltpu.VMEM((n, window + extra, rows, LANES), jnp.float32)

    count = len(blocks)
    return pl.pallas_call(
        functools.partial(
            step_kernel,
            cx=cx,
            cy=cy,
            steps=steps,
            sources=sources,
            window=window,
            dests=dests,
            fixed=fixed,
        ),
        out_shape=[
            jax.ShapeDtypeStruct(velocity.shape, jnp.float32),
            jax.ShapeDtypeStruct(stress.shape, jnp.float32),
            jax.ShapeDtypeStruct(memory.shape, jnp.float32),
        ],
        in_specs=[vmem] * (count + 1) + [smem],
        out_specs=[vmem] * 3,
        scratch_shapes=[
            frames(3, 4),
            frames(6, 4),
            frames(6, 0),
            frame,
            pltpu.VMEM((window // BLK, rows, LANES), jnp.float32),
            frame,
            frame,
            frame,
            frame,
            frame,
            frame,
            pltpu.SMEM((count * SUB, LANES), jnp.float32),
            pltpu.SemaphoreType.DMA((count,)),
        ],
        compiler_params=pltpu.CompilerParams(vmem_limit_bytes=40 << 20),
        name="steps",
    )(*blocks, table, place)


def solution(mesh):
    in_specs = (
        P(None, "we", "sn", None),
        P(None, "we", "sn", None),
        P(None, "we", "sn", None),
        P("we", "sn", None),
        P("we", "sn", None),
        P(),
        P("we", "sn", None),
        P("we", "sn", None, None),
    )
    out_specs = (P(None, "we", "sn", None), P(None, "we", "sn", None), P(None, "we", "sn", None))
    return jax.shard_map(shards, mesh=mesh, in_specs=in_specs, out_specs=out_specs, check_vma=False)
```

```python
import functools

import jax
import jax.numpy as jnp
from jax import lax
from jax.experimental import pallas as pl
from jax.experimental.pallas import tpu as pltpu
from jax.sharding import PartitionSpec as P

BLK = 4
BLKZ = 32
LANES = 128
SUB = 8

inner_coef = 9.0 / 8.0
outer_coef = 1.0 / 24.0
ratio = outer_coef / inner_coef
time_step = 0.08
friction = 0.4

VEL, STR, MEM, COD = 0, 3, 9, 15
FIELDS = 16
NORMAL = (0, 4, 5)


def round_up(value, step):
    return -(-value // step) * step


def pack_kernel(vel, stress, mem, code, scale, cell, amp, out, sem, *, field):
    copies = []
    for i, (at, part) in enumerate(((VEL, vel), (STR, stress), (MEM, mem))):
        to = out.at[pl.ds(at * field, part.shape[0]), :]
        copies.append(pltpu.make_async_copy(part, to, sem.at[i]))
        copies[-1].start()
    out[COD * field : (COD + 1) * field, :] = (code[...] + 1).astype(jnp.float32)
    lane = lax.broadcasted_iota(jnp.int32, (1, LANES), 1)
    here = FIELDS * field
    for i in range(scale.shape[1]):
        for j in range(scale.shape[0]):
            row = jnp.zeros((1, LANES), jnp.float32)
            for k in range(scale.shape[2]):
                row = jnp.where(lane // BLKZ == k, scale[j, i, k], row)
            out[here : here + 1, :] = row
            here += 1
    size = out.shape[0]
    if here < size - 1:
        out[here : size - 1, :] = jnp.zeros((size - 1 - here, LANES), jnp.float32)
    count, steps = amp.shape[2], amp.shape[3]
    row = jnp.zeros((1, LANES), jnp.float32)
    for k in range(count):
        row = jnp.where(lane == k, cell[0, 0, k].astype(jnp.float32), row)
        for t in range(steps):
            row = jnp.where(lane == count + k * steps + t, time_step * amp[0, 0, k, t], row)
    out[size - 1 : size, :] = row
    for copy in copies:
        copy.wait()


def step_kernel(*refs, cx, cy, steps, sources, window, dests, fixed):
    count = 3 * len(dests)
    blocks = refs[:count]
    table, place_ref = refs[count : count + 2]
    out_vel, out_str, out_mem = refs[count + 2 : count + 5]
    vel, stress, mem, codes, scales, buoy, lame, shear, decay, weight, cohesion, push_in = refs[
        count + 5 :
    ]
    field = cx * cy
    tail = FIELDS * field
    size = blocks[0].shape[0]
    margin = 4
    rows = codes.shape[1]

    me_we = place_ref[0]
    odd = lax.rem(place_ref[1], 2)
    if fixed is None:
        own = me_we * cx
    else:
        own = fixed

    zero = jnp.zeros((rows, LANES), jnp.float32)
    for p in (0, 1, window + 2, window + 3):
        for c in range(3):
            vel[c, p] = zero
            stress[c, p] = zero

    def base_plane(s):
        if fixed is None:
            return jnp.bitwise_xor(me_we, dests[s]) * cx
        return fixed - dests[s] * cx

    def place(block, plane, row):
        def piece(f, p):
            return block[pl.ds(f * field + p, cy, stride=cx), :]

        line = block[size - 1 : size, :]
        shape = (cy, LANES)
        spot = [jnp.broadcast_to(line[:, k : k + 1], shape) for k in range(sources * (1 + steps))]
        number = lax.broadcasted_iota(jnp.int32, shape, 0) * LANES
        number = (number + lax.broadcasted_iota(jnp.int32, shape, 1)).astype(jnp.float32)

        for p in range(cx):
            for c in range(3):
                vel[c, plane + p + 2, pl.ds(row, cy), :] = piece(VEL + c, p)
            for c in range(6):
                stress[c, plane + p + 2, pl.ds(row, cy), :] = piece(STR + c, p)
                mem[c, plane + p, pl.ds(row, cy), :] = piece(MEM + c, p)
            codes[plane + p, pl.ds(row, cy), :] = piece(COD, p)
            hits = [spot[k] == number + float(p * cy * LANES) for k in range(sources)]
            for t in range(steps):
                total = jnp.zeros(shape, jnp.float32)
                for k in range(sources):
                    total = total + jnp.where(hits[k], spot[sources + k * steps + t], 0.0)
                push_in[t, plane + p, pl.ds(row, cy), :] = total
        across = cy // BLK
        for i in range(cx // BLK):
            for j in range(across):
                at = tail + i * across + j
                wide = jnp.broadcast_to(block[at : at + 1, :], (BLK, LANES))
                scales[plane // BLK + i, pl.ds(row + j * BLK, BLK), :] = wide

    for s in range(len(dests)):
        plane = base_plane(s)
        center, outer, inner = blocks[3 * s : 3 * s + 3]
        place(center, plane, margin + cy)

        @pl.when(odd == 0)
        def _():
            place(outer, plane, margin)
            place(inner, plane, margin + 2 * cy)

        @pl.when(odd == 1)
        def _():
            place(inner, plane, margin)
            place(outer, plane, margin + 2 * cy)

    def properties(p, carry):
        for r in range(0, rows, SUB):
            index = codes[p, r : r + SUB, :].astype(jnp.int32)
            index = jnp.clip(index, 0, LANES - 1)

            def row_of(k):
                line = jnp.broadcast_to(table[k : k + 1, :], (SUB, LANES))
                return jnp.take_along_axis(line, index, axis=1)

            grow = scales[p // BLK, r : r + SUB, :]
            kept = row_of(3)
            buoy[p, r : r + SUB, :] = row_of(0)
            lame[p, r : r + SUB, :] = row_of(1) * grow
            shear[p, r : r + SUB, :] = row_of(2) * grow
            decay[p, r : r + SUB, :] = kept
            weight[p, r : r + SUB, :] = row_of(4)
            cohesion[p, r : r + SUB, :] = row_of(5)
        return carry

    lax.fori_loop(0, window, properties, 0)

    lane = lax.broadcasted_iota(jnp.int32, (SUB, LANES), 1)

    def deep(f, k):
        moved = pltpu.roll(f, (-k) % LANES, 1)
        return jnp.where((lane + k >= 0) & (lane + k < LANES), moved, 0.0)

    def z_back(f):
        return f - deep(f, -1), deep(f, 1) - deep(f, -2)

    def z_fore(f):
        return deep(f, 1) - f, deep(f, 2) - deep(f, -1)

    def add(*pairs):
        one, two = pairs[0]
        for a, b in pairs[1:]:
            one = one + a
            two = two + b
        return one - ratio * two

    def reader(ref, c, p, r):
        def at(dp, dr):
            return ref[c, p + 2 + dp, r + dr : r + dr + SUB, :]

        def x_fore():
            return at(1, 0) - at(0, 0), at(2, 0) - at(-1, 0)

        def x_back():
            return at(0, 0) - at(-1, 0), at(1, 0) - at(-2, 0)

        def y_fore():
            return at(0, 1) - at(0, 0), at(0, 2) - at(0, -1)

        def y_back():
            return at(0, 0) - at(0, -1), at(0, 1) - at(0, -2)

        return at, x_fore, x_back, y_fore, y_back

    def tiles(reach):
        need = cy + 2 * reach
        n = -(-need // SUB)
        start = margin + cy - reach
        return [start + SUB * i for i in range(n)]

    def planes(reach):
        need = min(cx + 2 * reach, window)
        if fixed is not None:
            return fixed - reach, cx + 2 * reach
        devices = window // cx
        need = max(
            min(w * cx + cx + reach, window) - max(w * cx - reach, 0) for w in range(devices)
        )
        return jnp.clip(own - reach, 0, window - need), need

    def velocity_phase(reach):
        first, n = planes(reach)

        def body(i, carry):
            p = first + i
            for r in tiles(reach):
                _, xx_fore, _, _, _ = reader(stress, 0, p, r)
                xz, _, xz_back, _, _ = reader(stress, 1, p, r)
                _, _, xy_xback, _, xy_yback = reader(stress, 2, p, r)
                yz, _, _, _, yz_back = reader(stress, 3, p, r)
                _, _, _, yy_fore, _ = reader(stress, 4, p, r)
                zz, _, _, _, _ = reader(stress, 5, p, r)
                push = buoy[p, r : r + SUB, :]
                forces = (
                    add(xx_fore(), xy_yback(), z_back(xz(0, 0))),
                    add(xy_xback(), yy_fore(), z_back(yz(0, 0))),
                    add(xz_back(), yz_back(), z_fore(zz(0, 0))),
                )
                for c in range(3):
                    vel[c, p + 2, r : r + SUB, :] = vel[c, p + 2, r : r + SUB, :] + push * forces[c]
            return carry

        lax.fori_loop(0, n, body, 0)

    def stress_phase(reach, t):
        first, n = planes(reach)

        def body(i, carry):
            p = first + i
            for j, r in enumerate(tiles(reach)):
                ve, _, ve_xback, ve_yfore, _ = reader(vel, 0, p, r)
                vn, vn_xfore, _, _, vn_yback = reader(vel, 1, p, r)
                vd, vd_xfore, _, vd_yfore, _ = reader(vel, 2, p, r)
                exx = add(ve_xback())
                eyy = add(vn_yback())
                ezz = add(z_back(vd(0, 0)))
                exz = add(z_fore(ve(0, 0)), vd_xfore())
                exy = add(ve_yfore(), vn_xfore())
                eyz = add(z_fore(vn(0, 0)), vd_yfore())
                mu = shear[p, r : r + SUB, :]
                twice = mu + mu
                bulk = lame[p, r : r + SUB, :] * (exx + eyy + ezz)
                moves = (
                    bulk + twice * exx,
                    mu * exz,
                    mu * exy,
                    mu * eyz,
                    bulk + twice * eyy,
                    bulk + twice * ezz,
                )
                keep = decay[p, r : r + SUB, :]
                gain = weight[p, r : r + SUB, :]
                source = push_in[t, p, r : r + SUB, :]
                trial = []
                rest = []
                for c in range(6):
                    old = mem[c, p, r : r + SUB, :]
                    new = keep * old + gain * moves[c]
                    rest.append(new)
                    now = stress[c, p + 2, r : r + SUB, :]
                    if c in NORMAL:
                        now = now + source
                    trial.append((now + moves[c]) - (0.5 * time_step) * (old + new))
                mean = (trial[0] + trial[4] + trial[5]) * (1.0 / 3.0)
                dxx, dyy, dzz = trial[0] - mean, trial[4] - mean, trial[5] - mean
                dxz, dxy, dyz = trial[1], trial[2], trial[3]
                second = 0.5 * (dxx * dxx + dyy * dyy + dzz * dzz) + (
                    dxz * dxz + dxy * dxy + dyz * dyz
                )
                soft = jnp.maximum(-mean, 0.0) + jnp.log(1.0 + jnp.exp(-jnp.abs(mean)))
                level = cohesion[p, r : r + SUB, :] + friction * soft
                scaled = second / (level * level)
                factor = lax.rsqrt(jnp.sqrt(1.0 + scaled * scaled))
                done = (
                    mean + factor * dxx,
                    factor * dxz,
                    factor * dxy,
                    factor * dyz,
                    mean + factor * dyy,
                    mean + factor * dzz,
                )
                if t == steps - 1:
                    lo = SUB * j
                    n_rows = min(SUB, cy - lo)
                    now_vel = (ve(0, 0), vn(0, 0), vd(0, 0))

                    def put(out, c, value):
                        at = c * field + lo * cx + i
                        out[pl.ds(at, n_rows, stride=cx), :] = value[:n_rows]

                    for c in range(3):
                        put(out_vel, c, now_vel[c])
                    for c in range(6):
                        put(out_str, c, done[c])
                        put(out_mem, c, rest[c])
                else:
                    for c in range(6):
                        stress[c, p + 2, r : r + SUB, :] = done[c]
                        mem[c, p, r : r + SUB, :] = rest[c]
            return carry

        lax.fori_loop(0, n, body, 0)

    for t in range(steps):
        left = 3 * (steps - 1 - t)
        velocity_phase(left + 2)
        stress_phase(left, t)


def shards(
    velocity, stress, memory, material_code, block_scale, material_table, source_cell, source_amp
):
    _, cx, cy, cz = velocity.shape
    sources, steps = source_amp.shape[2:]
    n_we, n_sn = lax.axis_size("we"), lax.axis_size("sn")
    reach = 3 * steps
    assert cz == LANES and cy >= reach and cx % BLK == 0 and cy % BLK == 0
    assert sources * (steps + 1) <= LANES

    used = FIELDS * cx * cy + (cx // BLK) * (cy // BLK) + 1
    vmem = pl.BlockSpec(memory_space=pltpu.VMEM)
    smem = pl.BlockSpec(memory_space=pltpu.SMEM)
    anywhere = pl.BlockSpec(memory_space=pl.ANY)

    def flat(x):
        return jnp.swapaxes(x, -3, -2).reshape(-1, LANES)

    own = pl.pallas_call(
        functools.partial(pack_kernel, field=cx * cy),
        out_shape=jax.ShapeDtypeStruct((round_up(used, SUB), LANES), jnp.float32),
        in_specs=[anywhere, anywhere, anywhere, vmem, smem, smem, smem],
        out_specs=vmem,
        scratch_shapes=[pltpu.SemaphoreType.DMA((3,))],
        name="pack",
    )(
        flat(velocity),
        flat(stress),
        flat(memory),
        flat(material_code),
        jnp.swapaxes(block_scale, 0, 1),
        source_cell,
        source_amp,
    )

    width = -(-reach // cx)
    everything = n_we <= 2 * width + 1 and n_we & (n_we - 1) == 0
    if everything:
        dests = list(range(n_we))
        window, fixed = n_we * cx, None
        moves = [[(i, i ^ k) for i in range(n_we)] for k in dests]
    else:
        dests = [0] + [sign * k for k in range(1, width + 1) for sign in (1, -1)]
        window, fixed = (2 * width + 1) * cx, width * cx
        moves = [[(i, i + k) for i in range(n_we) if 0 <= i + k < n_we] for k in dests]
    inner = [(i, i ^ 1) for i in range(n_sn) if i ^ 1 < n_sn]
    outer = [(i, i - 1 + 2 * (i % 2)) for i in range(n_sn)]
    outer = [(a, b) for a, b in outer if 0 <= b < n_sn]
    blocks = []
    for k, move in zip(dests, moves):
        block = own if k == 0 else lax.ppermute(own, "we", move)
        blocks += [block, lax.ppermute(block, "sn", outer), lax.ppermute(block, "sn", inner)]

    decay = material_table[3]
    per_step = time_step * inner_coef
    table = jnp.stack(
        [
            material_table[0] * per_step,
            material_table[1] * per_step,
            material_table[2] * per_step,
            decay,
            (1.0 - decay) * material_table[4] / time_step,
            material_table[5],
        ]
    )
    table = jnp.pad(table, ((0, 2), (1, LANES - 1 - table.shape[1])))

    place = jnp.stack([lax.axis_index("we"), lax.axis_index("sn")])

    margin = 4
    low = margin + cy - reach + 1
    rows = round_up(low + round_up(cy + 2 * reach - 2, SUB) + 2, SUB)
    frame = pltpu.VMEM((window, rows, LANES), jnp.float32)

    def frames(n, extra):
        return pltpu.VMEM((n, window + extra, rows, LANES), jnp.float32)

    count = len(blocks)
    outs = pl.pallas_call(
        functools.partial(
            step_kernel,
            cx=cx,
            cy=cy,
            steps=steps,
            sources=sources,
            window=window,
            dests=dests,
            fixed=fixed,
        ),
        out_shape=[
            jax.ShapeDtypeStruct((n * cx * cy, LANES), jnp.float32) for n in (3, 6, 6)
        ],
        in_specs=[vmem] * (count + 1) + [smem],
        out_specs=[vmem] * 3,
        scratch_shapes=[
            frames(3, 4),
            frames(6, 4),
            frames(6, 0),
            frame,
            pltpu.VMEM((window // BLK, rows, LANES), jnp.float32),
            frame,
            frame,
            frame,
            frame,
            frame,
            frame,
            frames(steps, 0),
        ],
        compiler_params=pltpu.CompilerParams(vmem_limit_bytes=40 << 20),
        name="steps",
    )(*blocks, table, place)
    return tuple(jnp.swapaxes(x.reshape(-1, cy, cx, cz), 1, 2) for x in outs)


def solution(mesh):
    in_specs = (
        P(None, "we", "sn", None),
        P(None, "we", "sn", None),
        P(None, "we", "sn", None),
        P("we", "sn", None),
        P("we", "sn", None),
        P(),
        P("we", "sn", None),
        P("we", "sn", None, None),
    )
    out_specs = (P(None, "we", "sn", None), P(None, "we", "sn", None), P(None, "we", "sn", None))
    return jax.shard_map(shards, mesh=mesh, in_specs=in_specs, out_specs=out_specs, check_vma=False)
```

```python
import functools

import jax
import jax.numpy as jnp
from jax import lax
from jax.experimental import pallas as pl
from jax.experimental.pallas import tpu as pltpu
from jax.sharding import PartitionSpec as P


BLK = 4
BLKZ = 32
LANES = 128
SUB = 8

inner_coef = 9.0 / 8.0
outer_coef = 1.0 / 24.0
ratio = outer_coef / inner_coef
time_step = 0.08
friction = 0.4

VEL, STR, MEM, COD = 0, 3, 9, 15
FIELDS = 16
NORMAL = (0, 4, 5)
UNROLL = 1


def round_up(value, step):
    return -(-value // step) * step


def pack_kernel(vel, stress, mem, code, scale, cell, amp, kinds, out, table, sem, *, field):
    copies = []
    for i, (at, part) in enumerate(((VEL, vel), (STR, stress), (MEM, mem))):
        to = out.at[pl.ds(at * field, part.shape[0]), :]
        copies.append(pltpu.make_async_copy(part, to, sem.at[i]))
        copies[-1].start()
    out[COD * field : (COD + 1) * field, :] = (code[...] + 1).astype(jnp.float32)
    lane = lax.broadcasted_iota(jnp.int32, (1, LANES), 1)
    here = FIELDS * field
    for i in range(scale.shape[1]):
        for j in range(scale.shape[0]):
            row = jnp.zeros((1, LANES), jnp.float32)
            for k in range(scale.shape[2]):
                row = jnp.where(lane // BLKZ == k, scale[j, i, k], row)
            out[here : here + 1, :] = row
            here += 1
    size = out.shape[0]
    if here < size - 1:
        out[here : size - 1, :] = jnp.zeros((size - 1 - here, LANES), jnp.float32)
    count, steps = amp.shape[2], amp.shape[3]
    row = jnp.zeros((1, LANES), jnp.float32)
    for k in range(count):
        row = jnp.where(lane == k, cell[0, 0, k].astype(jnp.float32), row)
        for t in range(steps):
            row = jnp.where(lane == count + k * steps + t, time_step * amp[0, 0, k, t], row)
    out[size - 1 : size, :] = row
    per_step = time_step * inner_coef
    lines = [jnp.zeros((1, LANES), jnp.float32) for _ in range(table.shape[0])]
    for k in range(kinds.shape[1]):
        decay = kinds[3, k]
        values = (
            kinds[0, k] * per_step,
            kinds[1, k] * per_step,
            kinds[2, k] * per_step,
            decay,
            (1.0 - decay) * kinds[4, k] * (1.0 / time_step),
            kinds[5, k],
        )
        for i, value in enumerate(values):
            lines[i] = jnp.where(lane == k + 1, value, lines[i])
    for i, line in enumerate(lines):
        table[i : i + 1, :] = line
    for copy in copies:
        copy.wait()


class Layout:
    def __init__(self, cx, cy, steps, sources, window, dests, fixed):
        self.cx, self.cy, self.steps, self.sources = cx, cy, steps, sources
        self.window, self.dests, self.fixed = window, tuple(dests), fixed
        self.field = cx * cy
        self.margin = 4
        low = self.margin + cy - 3 * steps + 1
        self.rows = round_up(low + round_up(cy + 6 * steps - 2, SUB) + 2, SUB)

    def base_plane(self, s, me):
        if self.fixed is None:
            return jnp.bitwise_xor(me, self.dests[s]) * self.cx
        return self.fixed - self.dests[s] * self.cx

    def tiles(self, reach):
        return self.margin + self.cy - reach, -(-(self.cy + 2 * reach) // SUB)

    def planes(self, reach, me):
        if self.fixed is not None:
            return self.fixed - reach, self.cx + 2 * reach
        own = [w * self.cx for w in range(self.window // self.cx)]
        need = max(
            min(w + self.cx + reach, self.window) - max(w - reach, 0) for w in own
        )
        return jnp.clip(me * self.cx - reach, 0, self.window - need), need


class State:
    def __init__(self, vel, stress, mem):
        self.vel, self.stress, self.mem = vel, stress, mem


def unpack(lay, block, table, state, props, push_in, plane, row, last_step):
    cx, cy, sources, steps = lay.cx, lay.cy, lay.sources, lay.steps
    shape = (cy, LANES)
    size = block.shape[0]

    def piece(f, p):
        return block[pl.ds(f * lay.field + p, cy, stride=cx), :]

    line = block[size - 1 : size, :]
    spot = [
        jnp.broadcast_to(line[:, k : k + 1], shape) for k in range(sources * (1 + steps))
    ]
    number = lax.broadcasted_iota(jnp.int32, shape, 0) * LANES
    number = (number + lax.broadcasted_iota(jnp.int32, shape, 1)).astype(jnp.float32)
    lines = [jnp.broadcast_to(table[k : k + 1, :], (SUB, LANES)) for k in range(6)]
    across = cy // BLK
    for i in range(cx // BLK):
        first = FIELDS * lay.field + i * across
        grow = jnp.concatenate(
            [
                jnp.broadcast_to(block[first + j : first + j + 1, :], (BLK, LANES))
                for j in range(across)
            ],
            axis=0,
        )
        for p in range(i * BLK, (i + 1) * BLK):
            for c in range(3):
                state.vel[c, plane + p + 2, pl.ds(row, cy), :] = piece(VEL + c, p)
            for c in range(6):
                state.stress[c, plane + p + 2, pl.ds(row, cy), :] = piece(STR + c, p)
                state.mem[c, plane + p, pl.ds(row, cy), :] = piece(MEM + c, p)
            code = jnp.clip(piece(COD, p).astype(jnp.int32), 0, LANES - 1)
            for lo in range(0, cy, SUB):
                n = min(SUB, cy - lo)
                index = code[lo : lo + n]
                for k in range(6):
                    value = jnp.take_along_axis(lines[k][:n], index, axis=1)
                    if k in (1, 2):
                        value = value * grow[lo : lo + n]
                    props[k, plane + p, pl.ds(row + lo, n), :] = value
            hits = [spot[k] == number + float(p * cy * LANES) for k in range(sources)]
            for t in range(last_step):
                total = jnp.zeros(shape, jnp.float32)
                for k in range(sources):
                    total = total + jnp.where(hits[k], spot[sources + k * steps + t], 0.0)
                push_in[t, plane + p, pl.ds(row, cy), :] = total


def deep(f, k):
    lane = lax.broadcasted_iota(jnp.int32, f.shape, 1)
    moved = pltpu.roll(f, (-k) % LANES, 1)
    keep = lane < LANES - k if k > 0 else lane >= -k
    return jnp.where(keep, moved, 0.0)


def z_back(f):
    return f - deep(f, -1), deep(f, 1) - deep(f, -2)


def z_fore(f):
    return deep(f, 1) - f, deep(f, 2) - deep(f, -1)


def add(*pairs):
    one, two = pairs[0]
    for a, b in pairs[1:]:
        one = one + a
        two = two + b
    return one - ratio * two


class Reader:
    def __init__(self, ref, c, p, r):
        self.ref, self.c, self.p, self.r = ref, c, p, r

    def at(self, dp=0, dr=0):
        return self.ref[self.c, self.p + 2 + dp, pl.ds(self.r + dr, SUB), :]

    def x_fore(self):
        return self.at(1) - self.at(0), self.at(2) - self.at(-1)

    def x_back(self):
        return self.at(0) - self.at(-1), self.at(1) - self.at(-2)

    def y_fore(self):
        return self.at(0, 1) - self.at(0, 0), self.at(0, 2) - self.at(0, -1)

    def y_back(self):
        return self.at(0, 0) - self.at(0, -1), self.at(0, 1) - self.at(0, -2)


def velocity_phase(old, new, props, first, n, start, count):
    def body(i, carry):
        p = first + i
        for r in [start + SUB * j for j in range(count)]:
            sxx, sxz, sxy, syz, syy, szz = [Reader(old.stress, c, p, r) for c in range(6)]
            push = props[0, p, pl.ds(r, SUB), :]
            forces = (
                add(sxx.x_fore(), sxy.y_back(), z_back(sxz.at())),
                add(sxy.x_back(), syy.y_fore(), z_back(syz.at())),
                add(sxz.x_back(), syz.y_back(), z_fore(szz.at())),
            )
            for c in range(3):
                now = old.vel[c, p + 2, pl.ds(r, SUB), :]
                new.vel[c, p + 2, pl.ds(r, SUB), :] = now + push * forces[c]
        return carry

    lax.fori_loop(0, n, body, 0, unroll=UNROLL)


def stress_phase(lay, old, new, props, push_in, t, first, n, start, count, outs=None):
    def body(i, carry):
        p = first + i
        for j in range(count):
            r = start + SUB * j
            here = pl.ds(r, SUB)
            ve, vn, vd = [Reader(new.vel, c, p, r) for c in range(3)]
            exx = add(ve.x_back())
            eyy = add(vn.y_back())
            ezz = add(z_back(vd.at()))
            exz = add(z_fore(ve.at()), vd.x_fore())
            exy = add(ve.y_fore(), vn.x_fore())
            eyz = add(z_fore(vn.at()), vd.y_fore())
            mu = props[2, p, here, :]
            twice = mu + mu
            bulk = props[1, p, here, :] * (exx + eyy + ezz)
            moves = (
                bulk + twice * exx,
                mu * exz,
                mu * exy,
                mu * eyz,
                bulk + twice * eyy,
                bulk + twice * ezz,
            )
            keep = props[3, p, here, :]
            gain = props[4, p, here, :]
            source = push_in[t, p, here, :]
            trial = []
            rest = []
            for c in range(6):
                before = old.mem[c, p, here, :]
                after = keep * before + gain * moves[c]
                rest.append(after)
                now = old.stress[c, p + 2, here, :]
                if c in NORMAL:
                    now = now + source
                trial.append((now + moves[c]) - (0.5 * time_step) * (before + after))
            mean = (trial[0] + trial[4] + trial[5]) * (1.0 / 3.0)
            dxx, dyy, dzz = trial[0] - mean, trial[4] - mean, trial[5] - mean
            dxz, dxy, dyz = trial[1], trial[2], trial[3]
            second = 0.5 * (dxx * dxx + dyy * dyy + dzz * dzz) + (
                dxz * dxz + dxy * dxy + dyz * dyz
            )
            soft = jnp.maximum(-mean, 0.0) + jnp.log(1.0 + jnp.exp(-jnp.abs(mean)))
            level = props[5, p, here, :] + friction * soft
            scaled = second / (level * level)
            factor = lax.rsqrt(jnp.sqrt(1.0 + scaled * scaled))
            done = (
                mean + factor * dxx,
                factor * dxz,
                factor * dxy,
                factor * dyz,
                mean + factor * dyy,
                mean + factor * dzz,
            )
            if outs is not None:
                lo = SUB * j
                n_rows = min(SUB, lay.cy - lo)

                def put(out, c, value):
                    at = c * lay.field + lo * lay.cx + i
                    out[pl.ds(at, n_rows, stride=lay.cx), :] = value[:n_rows]

                for c, part in enumerate((ve, vn, vd)):
                    put(outs[0], c, part.at())
                for c in range(6):
                    put(outs[1], c, done[c])
                    put(outs[2], c, rest[c])
            else:
                for c in range(6):
                    new.stress[c, p + 2, here, :] = done[c]
                    new.mem[c, p, here, :] = rest[c]
        return carry

    lax.fori_loop(0, n, body, 0, unroll=UNROLL)


def stage_kernel(*refs, lay, jobs, initial, final):
    blocks = refs[: len(jobs)]
    table, place = refs[len(jobs) : len(jobs) + 2]
    v0, s0, m0, v1, s1, m1, props, push_in = refs[-8:]
    zero, one = State(v0, s0, m0), State(v1, s1, m1)
    me, odd = place[0], lax.rem(place[1], 2)
    cy, margin, steps = lay.cy, lay.margin, lay.steps

    if initial:
        blank = jnp.zeros((lay.rows, LANES), jnp.float32)
        for p in (0, 1, lay.window + 2, lay.window + 3):
            for c in range(3):
                v1[c, p] = blank
                s0[c, p] = blank
                s1[c, p] = blank

    inner_row = jnp.where(odd == 0, margin + 2 * cy, margin)
    for block, (s, inner) in zip(blocks, jobs):
        plane = lay.base_plane(s, me)
        row, pushes = (inner_row, steps - 1) if inner else (margin + cy, steps)
        unpack(lay, block, table, zero, props, push_in, plane, row, pushes)
    if not final:
        return

    reach = 3 * steps - 1
    start, count = lay.tiles(reach)
    late = late_tiles(lay, reach)
    first, n = lay.planes(reach, me)
    end = start + lay.cy + 2 * reach
    at = jnp.where(odd == 0, end - SUB * (count - late), start)
    velocity_phase(zero, one, props, first, n, at, count - late)
    reach -= 2
    start, count = lay.tiles(reach)
    late = late_tiles(lay, reach)
    first, n = lay.planes(reach, me)
    end = start + lay.cy + 2 * reach
    at = jnp.where(odd == 0, end - SUB * (count - late), start)
    stress_phase(lay, zero, one, props, push_in, 0, first, n, at, count - late)


def late_tiles(lay, reach):
    into = 2 if reach == 3 * lay.steps - 1 else 4
    return -(-(reach + into) // SUB)


def late_kernel(*refs, lay):
    count = len(lay.dests)
    blocks = refs[:count]
    table, place = refs[count : count + 2]
    out_vel, out_str, out_mem, v0, s0, m0, v1, s1, m1, props, push_in = refs[count + 10 :]
    zero, one = State(v0, s0, m0), State(v1, s1, m1)
    me, odd = place[0], lax.rem(place[1], 2)
    cy, margin, steps = lay.cy, lay.margin, lay.steps

    outer_row = jnp.where(odd == 0, margin, margin + 2 * cy)
    for s in range(count):
        plane = lay.base_plane(s, me)
        unpack(lay, blocks[s], table, zero, props, push_in, plane, outer_row, steps - 1)

    reach = 3 * steps - 1
    start, _ = lay.tiles(reach)
    late = late_tiles(lay, reach)
    first, n = lay.planes(reach, me)
    at = jnp.where(odd == 0, start, start + cy + 2 * reach - SUB * late)
    velocity_phase(zero, one, props, first, n, at, late)
    reach -= 2
    start, _ = lay.tiles(reach)
    late = late_tiles(lay, reach)
    first, n = lay.planes(reach, me)
    at = jnp.where(odd == 0, start, start + cy + 2 * reach - SUB * late)
    stress_phase(lay, zero, one, props, push_in, 0, first, n, at, late)

    for t in range(1, steps):
        left = 3 * (steps - 1 - t)
        velocity_phase(one, one, props, *lay.planes(left + 2, me), *lay.tiles(left + 2))
        outs = (out_vel, out_str, out_mem) if t == steps - 1 else None
        stress_phase(
            lay, one, one, props, push_in, t, *lay.planes(left, me), *lay.tiles(left), outs
        )


def sees_all(n_we, width):
    return n_we <= 2 * width + 1 and n_we & (n_we - 1) == 0


def devices_in_view(n_we, width):
    return n_we if sees_all(n_we, width) else 2 * width + 1


def shards(
    velocity, stress, memory, material_code, block_scale, material_table, source_cell, source_amp
):
    _, cx, cy, cz = velocity.shape
    sources, steps = source_amp.shape[2:]
    n_we, n_sn = lax.axis_size("we"), lax.axis_size("sn")
    reach = 3 * steps
    assert cz == LANES and cy >= reach and cx % BLK == 0 and cy % BLK == 0
    assert sources * (steps + 1) <= LANES

    used = FIELDS * cx * cy + (cx // BLK) * (cy // BLK) + 1
    vmem = pl.BlockSpec(memory_space=pltpu.VMEM)
    smem = pl.BlockSpec(memory_space=pltpu.SMEM)
    anywhere = pl.BlockSpec(memory_space=pl.ANY)

    def flat(x):
        return jnp.swapaxes(x, -3, -2).reshape(-1, LANES)

    assert material_table.shape[1] < LANES
    own, table = pl.pallas_call(
        functools.partial(pack_kernel, field=cx * cy),
        out_shape=[
            jax.ShapeDtypeStruct((n, LANES), jnp.float32) for n in (round_up(used, SUB), SUB)
        ],
        in_specs=[anywhere, anywhere, anywhere, vmem, smem, smem, smem, smem],
        out_specs=[vmem, vmem],
        scratch_shapes=[pltpu.SemaphoreType.DMA((3,))],
        name="pack",
    )(
        flat(velocity),
        flat(stress),
        flat(memory),
        flat(material_code),
        jnp.swapaxes(block_scale, 0, 1),
        source_cell,
        source_amp,
        material_table,
    )

    width = -(-reach // cx)
    everything = sees_all(n_we, width)
    if everything:
        dests = list(range(n_we))
        window, fixed = n_we * cx, None
        moves = [[(i, i ^ k) for i in range(n_we)] for k in dests]
    else:
        dests = [0] + [sign * k for k in range(1, width + 1) for sign in (1, -1)]
        window, fixed = (2 * width + 1) * cx, width * cx
        moves = [[(i, i + k) for i in range(n_we) if 0 <= i + k < n_we] for k in dests]
    inner = [(i, i ^ 1) for i in range(n_sn) if i ^ 1 < n_sn]
    outer = [(i, i - 1 + 2 * (i % 2)) for i in range(n_sn)]
    outer = [(a, b) for a, b in outer if 0 <= b < n_sn]
    place = jnp.stack([lax.axis_index("we"), lax.axis_index("sn")])

    lay = Layout(cx, cy, steps, sources, window, dests, fixed)

    def frames(n, extra):
        return jax.ShapeDtypeStruct((n, window + extra, lay.rows, LANES), jnp.float32)

    state = [frames(3, 4), frames(6, 4), frames(6, 0)]
    state = state + state + [frames(6, 0), frames(steps, 0)]
    params = pltpu.CompilerParams(vmem_limit_bytes=24 << 20)
    centers, inners, outers = [], [], []
    for i, move in enumerate(moves):
        block = own if i == 0 else lax.ppermute(own, "we", move)
        centers.append(block)
        outers.append(lax.ppermute(block, "sn", outer))
        inners.append(lax.ppermute(block, "sn", inner))

    held = []
    last = len(dests) - 1
    assert last + 1 == devices_in_view(n_we, width)
    for i in range(last + 1):
        jobs = [(i, False)] + ([(i - 1, True)] if i > 0 else [])
        if i == last:
            jobs.append((i, True))
        parts = [(inners if inner else centers)[k] for k, inner in jobs]
        extra = len(parts) + 2
        held = pl.pallas_call(
            functools.partial(stage_kernel, lay=lay, jobs=jobs, initial=i == 0, final=i == last),
            out_shape=state,
            in_specs=[vmem] * (extra - 1) + [smem] + [vmem] * len(held),
            out_specs=[vmem] * len(state),
            input_output_aliases={extra + k: k for k in range(len(held))},
            compiler_params=params,
        )(*parts, table, place, *held)
    results = [jax.ShapeDtypeStruct((n * cx * cy, LANES), jnp.float32) for n in (3, 6, 6)]
    outs = pl.pallas_call(
        functools.partial(late_kernel, lay=lay),
        out_shape=results + state,
        in_specs=[vmem] * (len(outers) + 1) + [smem] + [vmem] * len(state),
        out_specs=[vmem] * (3 + len(state)),
        input_output_aliases={len(outers) + 2 + i: 3 + i for i in range(len(state))},
        compiler_params=params,
        name="late",
    )(*outers, table, place, *held)
    return tuple(jnp.swapaxes(x.reshape(-1, cy, cx, cz), 1, 2) for x in outs[:3])


def solution(mesh):
    in_specs = (
        P(None, "we", "sn", None),
        P(None, "we", "sn", None),
        P(None, "we", "sn", None),
        P("we", "sn", None),
        P("we", "sn", None),
        P(),
        P("we", "sn", None),
        P("we", "sn", None, None),
    )
    out_specs = (P(None, "we", "sn", None), P(None, "we", "sn", None), P(None, "we", "sn", None))

    def call(*args):
        step = jax.shard_map(
            shards, mesh=mesh, in_specs=in_specs, out_specs=out_specs, check_vma=False
        )
        return step(*args)

    return call
```

```python
import functools

import jax
import jax.numpy as jnp
from jax import lax
from jax.experimental import pallas as pl
from jax.experimental.pallas import tpu as pltpu
from jax.sharding import PartitionSpec as P


BLK = 4
BLKZ = 32
LANES = 128
SUB = 8

inner_coef = 9.0 / 8.0
outer_coef = 1.0 / 24.0
ratio = outer_coef / inner_coef
time_step = 0.08
friction = 0.4
half_step = 0.5 * time_step
largest = 3.0e38

VEL, STR, MEM, COD = 0, 3, 9, 15
FIELDS = 16
NORMAL = (0, 4, 5)
UNROLL = (8, 7)


def round_up(value, step):
    return -(-value // step) * step


def pack_kernel(vel, stress, mem, code, scale, cell, amp, kinds, out, table, sem, *, field):
    copies = []
    for i, (at, part) in enumerate(((VEL, vel), (STR, stress), (MEM, mem))):
        to = out.at[pl.ds(at * field, part.shape[0]), :]
        copies.append(pltpu.make_async_copy(part, to, sem.at[i]))
        copies[-1].start()
    out[COD * field : (COD + 1) * field, :] = (code[...] + 1).astype(jnp.float32)
    lane = lax.broadcasted_iota(jnp.int32, (1, LANES), 1)
    here = FIELDS * field
    for i in range(scale.shape[1]):
        for j in range(scale.shape[0]):
            row = jnp.zeros((1, LANES), jnp.float32)
            for k in range(scale.shape[2]):
                row = jnp.where(lane // BLKZ == k, scale[j, i, k], row)
            out[here : here + 1, :] = row
            here += 1
    size = out.shape[0]
    if here < size - 1:
        out[here : size - 1, :] = jnp.zeros((size - 1 - here, LANES), jnp.float32)
    count, steps = amp.shape[2], amp.shape[3]
    row = jnp.zeros((1, LANES), jnp.float32)
    for k in range(count):
        row = jnp.where(lane == k, cell[0, 0, k].astype(jnp.float32), row)
        for t in range(steps):
            row = jnp.where(lane == count + k * steps + t, time_step * amp[0, 0, k, t], row)
    out[size - 1 : size, :] = row
    per_step = time_step * inner_coef
    lines = [jnp.zeros((1, LANES), jnp.float32) for _ in range(table.shape[0])]
    for k in range(kinds.shape[1]):
        decay = kinds[3, k]
        values = (
            kinds[0, k] * per_step,
            kinds[1, k] * per_step,
            kinds[2, k] * per_step,
            decay,
            (1.0 - decay) * kinds[4, k] * (half_step / time_step),
            kinds[5, k],
        )
        for i, value in enumerate(values):
            lines[i] = jnp.where(lane == k + 1, value, lines[i])
    for i, line in enumerate(lines):
        table[i : i + 1, :] = line
    for copy in copies:
        copy.wait()


def divisor(n, top):
    return max(k for k in range(1, top + 1) if n % k == 0)


class Layout:
    def __init__(self, cx, cy, steps, sources, window, dests, fixed):
        self.cx, self.cy, self.steps, self.sources = cx, cy, steps, sources
        self.window, self.dests, self.fixed = window, tuple(dests), fixed
        self.field = cx * cy
        self.margin = 4
        low = self.margin + cy - 3 * steps + 1
        self.rows = round_up(low + round_up(cy + 6 * steps - 2, SUB) + 2, SUB)

    def base_plane(self, s, me):
        if self.fixed is None:
            return jnp.bitwise_xor(me, self.dests[s]) * self.cx
        return self.fixed - self.dests[s] * self.cx

    def tiles(self, reach):
        return self.margin + self.cy - reach, -(-(self.cy + 2 * reach) // SUB)

    def planes(self, reach, me):
        if self.fixed is not None:
            return self.fixed - reach, self.cx + 2 * reach
        own = [w * self.cx for w in range(self.window // self.cx)]
        need = max(
            min(w + self.cx + reach, self.window) - max(w - reach, 0) for w in own
        )
        need += need % 2 if need < self.window else 0
        return jnp.clip(me * self.cx - reach, 0, self.window - need), need


class State:
    def __init__(self, vel, stress, mem):
        self.vel, self.stress, self.mem = vel, stress, mem


def unpack(lay, block, table, state, props, push_in, plane, row, last_step):
    cx, cy, sources, steps = lay.cx, lay.cy, lay.sources, lay.steps
    shape = (cy, LANES)
    size = block.shape[0]

    def piece(f, p):
        return block[pl.ds(f * lay.field + p, cy, stride=cx), :]

    line = block[size - 1 : size, :]
    spot = [
        jnp.broadcast_to(line[:, k : k + 1], shape) for k in range(sources * (1 + steps))
    ]
    number = lax.broadcasted_iota(jnp.int32, shape, 0) * LANES
    number = (number + lax.broadcasted_iota(jnp.int32, shape, 1)).astype(jnp.float32)
    lines = [jnp.broadcast_to(table[k : k + 1, :], (SUB, LANES)) for k in range(6)]
    across = cy // BLK
    for i in range(cx // BLK):
        first = FIELDS * lay.field + i * across
        grow = jnp.concatenate(
            [
                jnp.broadcast_to(block[first + j : first + j + 1, :], (BLK, LANES))
                for j in range(across)
            ],
            axis=0,
        )
        for p in range(i * BLK, (i + 1) * BLK):
            for c in range(3):
                state.vel[c, plane + p + 2, pl.ds(row, cy), :] = piece(VEL + c, p)
            for c in range(6):
                state.stress[c, plane + p + 2, pl.ds(row, cy), :] = piece(STR + c, p)
                state.mem[c, plane + p, pl.ds(row, cy), :] = piece(MEM + c, p) * half_step
            code = jnp.clip(piece(COD, p).astype(jnp.int32), 0, LANES - 1)
            for lo in range(0, cy, SUB):
                n = min(SUB, cy - lo)
                index = code[lo : lo + n]
                for k in range(6):
                    value = jnp.take_along_axis(lines[k][:n], index, axis=1)
                    if k in (1, 2):
                        value = value * grow[lo : lo + n]
                    props[k, plane + p, pl.ds(row + lo, n), :] = value
            hits = [spot[k] == number + float(p * cy * LANES) for k in range(sources)]
            for t in range(last_step):
                total = jnp.zeros(shape, jnp.float32)
                for k in range(sources):
                    total = total + jnp.where(hits[k], spot[sources + k * steps + t], 0.0)
                push_in[t, plane + p, pl.ds(row, cy), :] = total


def deep(f, k):
    lane = lax.broadcasted_iota(jnp.int32, f.shape, 1)
    moved = pltpu.roll(f, (-k) % LANES, 1)
    keep = lane < LANES - k if k > 0 else lane >= -k
    return jnp.where(keep, moved, 0.0)


def z_back(f):
    return f - deep(f, -1), deep(f, 1) - deep(f, -2)


def z_fore(f):
    return deep(f, 1) - f, deep(f, 2) - deep(f, -1)


def add(*pairs):
    one, two = pairs[0]
    for a, b in pairs[1:]:
        one = one + a
        two = two + b
    return one - ratio * two


class Reader:
    def __init__(self, ref, c, p, r):
        self.ref, self.c, self.p, self.r = ref, c, p, r

    def at(self, dp=0, dr=0):
        return self.ref[self.c, self.p + 2 + dp, pl.ds(self.r + dr, SUB), :]

    def x_fore(self):
        return self.at(1) - self.at(0), self.at(2) - self.at(-1)

    def x_back(self):
        return self.at(0) - self.at(-1), self.at(1) - self.at(-2)

    def y_fore(self):
        return self.at(0, 1) - self.at(0, 0), self.at(0, 2) - self.at(0, -1)

    def y_back(self):
        return self.at(0, 0) - self.at(0, -1), self.at(0, 1) - self.at(0, -2)


def velocity_phase(old, new, props, first, n, start, count):
    def body(i, carry):
        p = first + i
        for r in [start + SUB * j for j in range(count)]:
            sxx, sxz, sxy, syz, syy, szz = [Reader(old.stress, c, p, r) for c in range(6)]
            push = props[0, p, pl.ds(r, SUB), :]
            forces = (
                add(sxx.x_fore(), sxy.y_back(), z_back(sxz.at())),
                add(sxy.x_back(), syy.y_fore(), z_back(syz.at())),
                add(sxz.x_back(), syz.y_back(), z_fore(szz.at())),
            )
            for c in range(3):
                now = old.vel[c, p + 2, pl.ds(r, SUB), :]
                new.vel[c, p + 2, pl.ds(r, SUB), :] = now + push * forces[c]
        return carry

    lax.fori_loop(0, n, body, 0, unroll=divisor(n, UNROLL[0]))


def stress_phase(lay, old, new, props, push_in, t, first, n, start, count, outs=None):
    def body(i, carry):
        p = first + i
        for j in range(count):
            r = start + SUB * j
            here = pl.ds(r, SUB)
            ve, vn, vd = [Reader(new.vel, c, p, r) for c in range(3)]
            exx = add(ve.x_back())
            eyy = add(vn.y_back())
            ezz = add(z_back(vd.at()))
            exz = add(z_fore(ve.at()), vd.x_fore())
            exy = add(ve.y_fore(), vn.x_fore())
            eyz = add(z_fore(vn.at()), vd.y_fore())
            mu = props[2, p, here, :]
            twice = mu + mu
            bulk = props[1, p, here, :] * (exx + eyy + ezz)
            moves = (
                bulk + twice * exx,
                mu * exz,
                mu * exy,
                mu * eyz,
                bulk + twice * eyy,
                bulk + twice * ezz,
            )
            keep = props[3, p, here, :]
            gain = props[4, p, here, :]
            source = push_in[t, p, here, :]
            trial = []
            rest = []
            for c in range(6):
                before = old.mem[c, p, here, :]
                after = keep * before + gain * moves[c]
                rest.append(after)
                now = old.stress[c, p + 2, here, :]
                if c in NORMAL:
                    now = now + source
                trial.append((now + moves[c]) - (before + after))
            mean = (trial[0] + trial[4] + trial[5]) * (1.0 / 3.0)
            dxx, dyy, dzz = trial[0] - mean, trial[4] - mean, trial[5] - mean
            dxz, dxy, dyz = trial[1], trial[2], trial[3]
            second = 0.5 * (dxx * dxx + dyy * dyy + dzz * dzz) + (
                dxz * dxz + dxy * dxy + dyz * dyz
            )
            soft = jnp.maximum(-mean, 0.0) + jnp.log(1.0 + jnp.exp(-jnp.abs(mean)))
            level = props[5, p, here, :] + friction * soft
            scaled = second / (level * level)
            grown = jnp.minimum(1.0 + scaled * scaled, largest)
            factor = lax.rsqrt(grown * lax.rsqrt(grown))
            done = (
                mean + factor * dxx,
                factor * dxz,
                factor * dxy,
                factor * dyz,
                mean + factor * dyy,
                mean + factor * dzz,
            )
            if outs is not None:
                lo = SUB * j
                n_rows = min(SUB, lay.cy - lo)

                def put(out, c, value):
                    at = c * lay.field + lo * lay.cx + i
                    out[pl.ds(at, n_rows, stride=lay.cx), :] = value[:n_rows]

                for c, part in enumerate((ve, vn, vd)):
                    put(outs[0], c, part.at())
                for c in range(6):
                    put(outs[1], c, done[c])
                    put(outs[2], c, rest[c] * (1.0 / half_step))
            else:
                for c in range(6):
                    new.stress[c, p + 2, here, :] = done[c]
                    new.mem[c, p, here, :] = rest[c]
        return carry

    lax.fori_loop(0, n, body, 0, unroll=divisor(n, UNROLL[1]))


CENTER, INNER, OUTER = 0, 1, 2
EARLY_STEPS = 2


def unpack_jobs(lay, blocks, jobs, table, state, props, push_in, me, odd):
    cy, margin, steps = lay.cy, lay.margin, lay.steps
    rows = (
        margin + cy,
        jnp.where(odd == 0, margin + 2 * cy, margin),
        jnp.where(odd == 0, margin, margin + 2 * cy),
    )
    for block, (s, kind) in zip(blocks, jobs):
        plane = lay.base_plane(s, me)
        pushes = steps if kind == CENTER else steps - 1
        unpack(lay, block, table, state, props, push_in, plane, rows[kind], pushes)


def states_of(refs):
    return [State(*refs[i : i + 3]) for i in range(0, len(refs), 3)]


def stage_kernel(*refs, lay, jobs, initial, final, held):
    blocks = refs[: len(jobs)]
    table, place = refs[len(jobs) : len(jobs) + 2]
    refs = refs[-held:]
    props, push_in = refs[:2]
    states = states_of(refs[2:])
    me, odd = place[0], lax.rem(place[1], 2)

    if initial:
        blank = jnp.zeros((lay.rows, LANES), jnp.float32)
        for p in (0, 1, lay.window + 2, lay.window + 3):
            for c in range(3):
                for i, state in enumerate(states):
                    if i > 0:
                        state.vel[c, p] = blank
                    state.stress[c, p] = blank
    unpack_jobs(lay, blocks, jobs, table, states[0], props, push_in, me, odd)
    if not final:
        return

    for t in range(len(states) - 1):
        for k in (0, 1):
            reach, late = split(lay, t, k)
            start, count = lay.tiles(reach)
            first, n = lay.planes(reach, me)
            end = start + lay.cy + 2 * reach
            at = jnp.where(odd == 0, end - SUB * (count - late), start)
            part = (first, n, at, count - late)
            if k == 0:
                velocity_phase(states[t], states[t + 1], props, *part)
            else:
                stress_phase(lay, states[t], states[t + 1], props, push_in, t, *part)


def split(lay, t, k):
    reach = 3 * (lay.steps - 1 - t) + (2 if k == 0 else 0)
    return reach, -(-(reach + 4 * t + 2 * k + 2) // SUB)


def late_kernel(*refs, lay, jobs, held):
    count = len(jobs)
    blocks = refs[:count]
    table, place = refs[count : count + 2]
    outs = refs[count + 2 + held : count + 5 + held]
    refs = refs[-held:]
    props, push_in = refs[:2]
    states = states_of(refs[2:])
    me, odd = place[0], lax.rem(place[1], 2)
    unpack_jobs(lay, blocks, jobs, table, states[0], props, push_in, me, odd)

    for t in range(lay.steps):
        for k in (0, 1):
            reach, late = split(lay, t, k)
            start, count = lay.tiles(reach)
            first, n = lay.planes(reach, me)
            if t + 1 < len(states):
                old, new = states[t], states[t + 1]
                end = start + lay.cy + 2 * reach
                part = (first, n, jnp.where(odd == 0, start, end - SUB * late), late)
            else:
                old = new = states[-1]
                part = (first, n, start, count)
            if k == 0:
                velocity_phase(old, new, props, *part)
            else:
                final = outs if t == lay.steps - 1 else None
                stress_phase(lay, old, new, props, push_in, t, *part, final)


def sees_all(n_we, width):
    return n_we <= 2 * width + 1 and n_we & (n_we - 1) == 0


def devices_in_view(n_we, width):
    return n_we if sees_all(n_we, width) else 2 * width + 1


def shards(
    velocity, stress, memory, material_code, block_scale, material_table, source_cell, source_amp
):
    _, cx, cy, cz = velocity.shape
    sources, steps = source_amp.shape[2:]
    n_we, n_sn = lax.axis_size("we"), lax.axis_size("sn")
    reach = 3 * steps
    assert cz == LANES and cy >= reach and cx % BLK == 0 and cy % BLK == 0
    assert sources * (steps + 1) <= LANES

    used = FIELDS * cx * cy + (cx // BLK) * (cy // BLK) + 1
    vmem = pl.BlockSpec(memory_space=pltpu.VMEM)
    smem = pl.BlockSpec(memory_space=pltpu.SMEM)
    anywhere = pl.BlockSpec(memory_space=pl.ANY)

    def flat(x):
        return jnp.swapaxes(x, -3, -2).reshape(-1, LANES)

    assert material_table.shape[1] < LANES
    own, table = pl.pallas_call(
        functools.partial(pack_kernel, field=cx * cy),
        out_shape=[
            jax.ShapeDtypeStruct((n, LANES), jnp.float32) for n in (round_up(used, SUB), SUB)
        ],
        in_specs=[anywhere, anywhere, anywhere, vmem, smem, smem, smem, smem],
        out_specs=[vmem, vmem],
        scratch_shapes=[pltpu.SemaphoreType.DMA((3,))],
        name="pack",
    )(
        flat(velocity),
        flat(stress),
        flat(memory),
        flat(material_code),
        jnp.swapaxes(block_scale, 0, 1),
        source_cell,
        source_amp,
        material_table,
    )

    width = -(-reach // cx)
    everything = sees_all(n_we, width)
    if everything:
        dests = list(range(n_we))
        window, fixed = n_we * cx, None
        moves = [[(i, i ^ k) for i in range(n_we)] for k in dests]
    else:
        dests = [0] + [sign * k for k in range(1, width + 1) for sign in (1, -1)]
        window, fixed = (2 * width + 1) * cx, width * cx
        moves = [[(i, i + k) for i in range(n_we) if 0 <= i + k < n_we] for k in dests]
    inner = [(i, i ^ 1) for i in range(n_sn) if i ^ 1 < n_sn]
    outer = [(i, i - 1 + 2 * (i % 2)) for i in range(n_sn)]
    outer = [(a, b) for a, b in outer if 0 <= b < n_sn]
    place = jnp.stack([lax.axis_index("we"), lax.axis_index("sn")])

    lay = Layout(cx, cy, steps, sources, window, dests, fixed)

    def frames(n, extra):
        return jax.ShapeDtypeStruct((n, window + extra, lay.rows, LANES), jnp.float32)

    early = min(EARLY_STEPS, steps - 1)
    state = [frames(6, 0), frames(steps, 0)]
    state += (early + 1) * [frames(3, 4), frames(6, 4), frames(6, 0)]
    params = pltpu.CompilerParams(vmem_limit_bytes=16 << 20)
    ready = {}
    for i, move in enumerate(moves):
        block = own if i == 0 else lax.ppermute(own, "we", move)
        ready[i, CENTER] = block
        ready[i, OUTER] = lax.ppermute(block, "sn", outer)
        ready[i, INNER] = lax.ppermute(block, "sn", inner)

    held = []
    last = len(dests) - 1
    assert last + 1 == devices_in_view(n_we, width)
    for i in range(last + 1):
        jobs = [(i, CENTER)]
        if i > 0:
            jobs.append((i - 1, INNER))
        if i == last:
            jobs.append((i, INNER))
        elif i > 0:
            jobs.append((i - 1, OUTER))
        parts = [ready.pop(job) if job[1] else ready[job] for job in jobs]
        extra = len(parts) + 2
        held = pl.pallas_call(
            functools.partial(
                stage_kernel,
                lay=lay,
                jobs=jobs,
                initial=i == 0,
                final=i == last,
                held=len(state),
            ),
            out_shape=state,
            in_specs=[vmem] * (extra - 1) + [smem] + [vmem] * len(held),
            out_specs=[vmem] * len(state),
            input_output_aliases={extra + k: k for k in range(len(held))},
            compiler_params=params,
        )(*parts, table, place, *held)
    jobs = [job for job in ready if job[1] != CENTER]
    parts = [ready[job] for job in jobs]
    extra = len(parts) + 2
    results = [jax.ShapeDtypeStruct((n * cx * cy, LANES), jnp.float32) for n in (3, 6, 6)]
    outs = pl.pallas_call(
        functools.partial(late_kernel, lay=lay, jobs=jobs, held=len(state)),
        out_shape=results + state,
        in_specs=[vmem] * (extra - 1) + [smem] + [vmem] * len(state),
        out_specs=[vmem] * (3 + len(state)),
        input_output_aliases={extra + i: 3 + i for i in range(len(state))},
        compiler_params=params,
        name="late",
    )(*parts, table, place, *held)
    return tuple(jnp.swapaxes(x.reshape(-1, cy, cx, cz), 1, 2) for x in outs[:3])


def solution(mesh):
    in_specs = (
        P(None, "we", "sn", None),
        P(None, "we", "sn", None),
        P(None, "we", "sn", None),
        P("we", "sn", None),
        P("we", "sn", None),
        P(),
        P("we", "sn", None),
        P("we", "sn", None, None),
    )
    out_specs = (P(None, "we", "sn", None), P(None, "we", "sn", None), P(None, "we", "sn", None))

    def call(*args):
        step = jax.shard_map(
            shards, mesh=mesh, in_specs=in_specs, out_specs=out_specs, check_vma=False
        )
        return step(*args)

    return call
```

```python
import functools

import jax
import jax.numpy as jnp
from jax import lax
from jax.experimental import pallas as pl
from jax.experimental.pallas import tpu as pltpu
from jax.sharding import PartitionSpec as P


BLK = 4
BLKZ = 32
LANES = 128
SUB = 8

inner_coef = 9.0 / 8.0
outer_coef = 1.0 / 24.0
ratio = outer_coef / inner_coef
time_step = 0.08
friction = 0.4
half_step = 0.5 * time_step
largest = 3.0e38

VEL, STR, MEM, COD = 0, 3, 9, 15
FIELDS = 16
SPLIT = 8
WHOLE, FIRST, SECOND = 0, 1, 2
HELD = (range(FIELDS), range(SPLIT), range(SPLIT, FIELDS))
NORMAL = (0, 4, 5)
UNROLL = (16, 14)


def round_up(value, step):
    return -(-value // step) * step


def pack_kernel(vel, stress, mem, code, scale, cell, amp, kinds, out, table, sem, *, field):
    copies = []
    for i, (at, part) in enumerate(((VEL, vel), (STR, stress), (MEM, mem))):
        to = out.at[pl.ds(at * field, part.shape[0]), :]
        copies.append(pltpu.make_async_copy(part, to, sem.at[i]))
        copies[-1].start()
    out[COD * field : (COD + 1) * field, :] = (code[...] + 1).astype(jnp.float32)
    lane = lax.broadcasted_iota(jnp.int32, (1, LANES), 1)
    here = FIELDS * field
    for i in range(scale.shape[1]):
        for j in range(scale.shape[0]):
            row = jnp.zeros((1, LANES), jnp.float32)
            for k in range(scale.shape[2]):
                row = jnp.where(lane // BLKZ == k, scale[j, i, k], row)
            out[here : here + 1, :] = row
            here += 1
    size = out.shape[0]
    if here < size - 1:
        out[here : size - 1, :] = jnp.zeros((size - 1 - here, LANES), jnp.float32)
    count, steps = amp.shape[2], amp.shape[3]
    row = jnp.zeros((1, LANES), jnp.float32)
    for k in range(count):
        row = jnp.where(lane == k, cell[0, 0, k].astype(jnp.float32), row)
        for t in range(steps):
            row = jnp.where(lane == count + k * steps + t, time_step * amp[0, 0, k, t], row)
    out[size - 1 : size, :] = row
    per_step = time_step * inner_coef
    lines = [jnp.zeros((1, LANES), jnp.float32) for _ in range(table.shape[0])]
    for k in range(kinds.shape[1]):
        decay = kinds[3, k]
        values = (
            kinds[0, k] * per_step,
            kinds[1, k] * per_step,
            kinds[2, k] * per_step,
            decay,
            (1.0 - decay) * kinds[4, k] * (half_step / time_step),
            kinds[5, k],
        )
        for i, value in enumerate(values):
            lines[i] = jnp.where(lane == k + 1, value, lines[i])
    for i, line in enumerate(lines):
        table[i : i + 1, :] = line
    for copy in copies:
        copy.wait()


def divisor(n, top):
    return max(k for k in range(1, top + 1) if n % k == 0)


class Layout:
    def __init__(self, cx, cy, steps, sources, window, dests, fixed):
        self.cx, self.cy, self.steps, self.sources = cx, cy, steps, sources
        self.window, self.dests, self.fixed = window, tuple(dests), fixed
        self.field = cx * cy
        self.margin = 4
        low = self.margin + cy - 3 * steps + 1
        self.rows = round_up(low + round_up(cy + 6 * steps - 2, SUB) + 2, SUB)

    def base_plane(self, s, me):
        if self.fixed is None:
            return jnp.bitwise_xor(me, self.dests[s]) * self.cx
        return self.fixed - self.dests[s] * self.cx

    def tiles(self, reach):
        return self.margin + self.cy - reach, -(-(self.cy + 2 * reach) // SUB)

    def planes(self, reach, me):
        if self.fixed is not None:
            return self.fixed - reach, self.cx + 2 * reach
        own = [w * self.cx for w in range(self.window // self.cx)]
        need = max(
            min(w + self.cx + reach, self.window) - max(w - reach, 0) for w in own
        )
        need += need % 2 if need < self.window else 0
        return jnp.clip(me * self.cx - reach, 0, self.window - need), need


class State:
    def __init__(self, vel, stress, mem):
        self.vel, self.stress, self.mem = vel, stress, mem


def unpack(lay, block, part, table, state, props, push_in, plane, row, last_step):
    cx, cy, sources, steps = lay.cx, lay.cy, lay.sources, lay.steps
    shape = (cy, LANES)
    size = block.shape[0]

    held = HELD[part]

    def piece(f, p):
        return block[pl.ds((f - held.start) * lay.field + p, cy, stride=cx), :]

    def copy_fields(p):
        for c in range(3):
            if VEL + c in held:
                state.vel[c, plane + p + 2, pl.ds(row, cy), :] = piece(VEL + c, p)
        for c in range(6):
            if STR + c in held:
                state.stress[c, plane + p + 2, pl.ds(row, cy), :] = piece(STR + c, p)
            if MEM + c in held:
                state.mem[c, plane + p, pl.ds(row, cy), :] = piece(MEM + c, p) * half_step

    if COD not in held:
        for p in range(cx):
            copy_fields(p)
        return

    line = block[size - 1 : size, :]
    spot = [
        jnp.broadcast_to(line[:, k : k + 1], shape) for k in range(sources * (1 + steps))
    ]
    number = lax.broadcasted_iota(jnp.int32, shape, 0) * LANES
    number = (number + lax.broadcasted_iota(jnp.int32, shape, 1)).astype(jnp.float32)
    lines = [jnp.broadcast_to(table[k : k + 1, :], (SUB, LANES)) for k in range(6)]
    across = cy // BLK
    for i in range(cx // BLK):
        first = len(held) * lay.field + i * across
        grow = jnp.concatenate(
            [
                jnp.broadcast_to(block[first + j : first + j + 1, :], (BLK, LANES))
                for j in range(across)
            ],
            axis=0,
        )
        for p in range(i * BLK, (i + 1) * BLK):
            copy_fields(p)
            code = jnp.clip(piece(COD, p).astype(jnp.int32), 0, LANES - 1)
            for lo in range(0, cy, SUB):
                n = min(SUB, cy - lo)
                index = code[lo : lo + n]
                for k in range(6):
                    value = jnp.take_along_axis(lines[k][:n], index, axis=1)
                    if k in (1, 2):
                        value = value * grow[lo : lo + n]
                    props[k, plane + p, pl.ds(row + lo, n), :] = value
            hits = [spot[k] == number + float(p * cy * LANES) for k in range(sources)]
            for t in range(last_step):
                total = jnp.zeros(shape, jnp.float32)
                for k in range(sources):
                    total = total + jnp.where(hits[k], spot[sources + k * steps + t], 0.0)
                push_in[t, plane + p, pl.ds(row, cy), :] = total


def deep(f, k):
    lane = lax.broadcasted_iota(jnp.int32, f.shape, 1)
    moved = pltpu.roll(f, (-k) % LANES, 1)
    keep = lane < LANES - k if k > 0 else lane >= -k
    return jnp.where(keep, moved, 0.0)


def z_back(f):
    return f - deep(f, -1), deep(f, 1) - deep(f, -2)


def z_fore(f):
    return deep(f, 1) - f, deep(f, 2) - deep(f, -1)


def add(*pairs):
    one, two = pairs[0]
    for a, b in pairs[1:]:
        one = one + a
        two = two + b
    return one - ratio * two


class Reader:
    def __init__(self, ref, c, p, r):
        self.ref, self.c, self.p, self.r = ref, c, p, r

    def at(self, dp=0, dr=0):
        return self.ref[self.c, self.p + 2 + dp, pl.ds(self.r + dr, SUB), :]

    def x_fore(self):
        return self.at(1) - self.at(0), self.at(2) - self.at(-1)

    def x_back(self):
        return self.at(0) - self.at(-1), self.at(1) - self.at(-2)

    def y_fore(self):
        return self.at(0, 1) - self.at(0, 0), self.at(0, 2) - self.at(0, -1)

    def y_back(self):
        return self.at(0, 0) - self.at(0, -1), self.at(0, 1) - self.at(0, -2)


def velocity_phase(old, new, props, first, n, start, count):
    def body(i, carry):
        p = first + i
        for r in [start + SUB * j for j in range(count)]:
            sxx, sxz, sxy, syz, syy, szz = [Reader(old.stress, c, p, r) for c in range(6)]
            push = props[0, p, pl.ds(r, SUB), :]
            forces = (
                add(sxx.x_fore(), sxy.y_back(), z_back(sxz.at())),
                add(sxy.x_back(), syy.y_fore(), z_back(syz.at())),
                add(sxz.x_back(), syz.y_back(), z_fore(szz.at())),
            )
            for c in range(3):
                now = old.vel[c, p + 2, pl.ds(r, SUB), :]
                new.vel[c, p + 2, pl.ds(r, SUB), :] = now + push * forces[c]
        return carry

    lax.fori_loop(0, n, body, 0, unroll=divisor(n, UNROLL[0]))


def stress_phase(lay, old, new, props, push_in, t, first, n, start, count, outs=None):
    def body(i, carry):
        p = first + i
        for j in range(count):
            r = start + SUB * j
            here = pl.ds(r, SUB)
            ve, vn, vd = [Reader(new.vel, c, p, r) for c in range(3)]
            exx = add(ve.x_back())
            eyy = add(vn.y_back())
            ezz = add(z_back(vd.at()))
            exz = add(z_fore(ve.at()), vd.x_fore())
            exy = add(ve.y_fore(), vn.x_fore())
            eyz = add(z_fore(vn.at()), vd.y_fore())
            mu = props[2, p, here, :]
            twice = mu + mu
            bulk = props[1, p, here, :] * (exx + eyy + ezz)
            moves = (
                bulk + twice * exx,
                mu * exz,
                mu * exy,
                mu * eyz,
                bulk + twice * eyy,
                bulk + twice * ezz,
            )
            keep = props[3, p, here, :]
            gain = props[4, p, here, :]
            source = push_in[t, p, here, :]
            trial = []
            rest = []
            for c in range(6):
                before = old.mem[c, p, here, :]
                after = keep * before + gain * moves[c]
                rest.append(after)
                now = old.stress[c, p + 2, here, :]
                if c in NORMAL:
                    now = now + source
                trial.append((now + moves[c]) - (before + after))
            mean = (trial[0] + trial[4] + trial[5]) * (1.0 / 3.0)
            dxx, dyy, dzz = trial[0] - mean, trial[4] - mean, trial[5] - mean
            dxz, dxy, dyz = trial[1], trial[2], trial[3]
            second = 0.5 * (dxx * dxx + dyy * dyy + dzz * dzz) + (
                dxz * dxz + dxy * dxy + dyz * dyz
            )
            soft = jnp.maximum(-mean, 0.0) + jnp.log(1.0 + jnp.exp(-jnp.abs(mean)))
            level = props[5, p, here, :] + friction * soft
            scaled = second / (level * level)
            grown = jnp.minimum(1.0 + scaled * scaled, largest)
            factor = lax.rsqrt(grown * lax.rsqrt(grown))
            done = (
                mean + factor * dxx,
                factor * dxz,
                factor * dxy,
                factor * dyz,
                mean + factor * dyy,
                mean + factor * dzz,
            )
            if outs is not None:
                lo = SUB * j
                n_rows = min(SUB, lay.cy - lo)

                def put(out, c, value):
                    at = c * lay.field + lo * lay.cx + i
                    out[pl.ds(at, n_rows, stride=lay.cx), :] = value[:n_rows]

                for c, part in enumerate((ve, vn, vd)):
                    put(outs[0], c, part.at())
                for c in range(6):
                    put(outs[1], c, done[c])
                    put(outs[2], c, rest[c] * (1.0 / half_step))
            else:
                for c in range(6):
                    new.stress[c, p + 2, here, :] = done[c]
                    new.mem[c, p, here, :] = rest[c]
        return carry

    lax.fori_loop(0, n, body, 0, unroll=divisor(n, UNROLL[1]))


CENTER, INNER, OUTER = 0, 1, 2
EARLY_STEPS = 2


def unpack_jobs(lay, blocks, jobs, table, state, props, push_in, me, odd):
    cy, margin, steps = lay.cy, lay.margin, lay.steps
    rows = (
        margin + cy,
        jnp.where(odd == 0, margin + 2 * cy, margin),
        jnp.where(odd == 0, margin, margin + 2 * cy),
    )
    for block, (s, kind, part) in zip(blocks, jobs):
        plane = lay.base_plane(s, me)
        pushes = steps if kind == CENTER else steps - 1
        unpack(lay, block, part, table, state, props, push_in, plane, rows[kind], pushes)


def states_of(refs):
    return [State(*refs[i : i + 3]) for i in range(0, len(refs), 3)]


def stage_kernel(*refs, lay, jobs, initial, final, held):
    blocks = refs[: len(jobs)]
    table, place = refs[len(jobs) : len(jobs) + 2]
    refs = refs[-held:]
    props, push_in = refs[:2]
    states = states_of(refs[2:])
    me, odd = place[0], lax.rem(place[1], 2)

    if initial:
        blank = jnp.zeros((lay.rows, LANES), jnp.float32)
        for p in (0, 1, lay.window + 2, lay.window + 3):
            for c in range(3):
                for i, state in enumerate(states):
                    if i > 0:
                        state.vel[c, p] = blank
                    state.stress[c, p] = blank
    unpack_jobs(lay, blocks, jobs, table, states[0], props, push_in, me, odd)
    if not final:
        return

    for t in range(len(states) - 1):
        for k in (0, 1):
            reach, late = split(lay, t, k)
            start, count = lay.tiles(reach)
            first, n = lay.planes(reach, me)
            end = start + lay.cy + 2 * reach
            at = jnp.where(odd == 0, end - SUB * (count - late), start)
            part = (first, n, at, count - late)
            if k == 0:
                velocity_phase(states[t], states[t + 1], props, *part)
            else:
                stress_phase(lay, states[t], states[t + 1], props, push_in, t, *part)


def split(lay, t, k):
    reach = 3 * (lay.steps - 1 - t) + (2 if k == 0 else 0)
    return reach, -(-(reach + 4 * t + 2 * k + 2) // SUB)


def late_kernel(*refs, lay, jobs, held):
    count = len(jobs)
    blocks = refs[:count]
    table, place = refs[count : count + 2]
    outs = refs[count + 2 + held : count + 5 + held]
    refs = refs[-held:]
    props, push_in = refs[:2]
    states = states_of(refs[2:])
    me, odd = place[0], lax.rem(place[1], 2)
    unpack_jobs(lay, blocks, jobs, table, states[0], props, push_in, me, odd)

    for t in range(lay.steps):
        for k in (0, 1):
            reach, late = split(lay, t, k)
            start, count = lay.tiles(reach)
            first, n = lay.planes(reach, me)
            if t + 1 < len(states):
                old, new = states[t], states[t + 1]
                end = start + lay.cy + 2 * reach
                part = (first, n, jnp.where(odd == 0, start, end - SUB * late), late)
            else:
                old = new = states[-1]
                part = (first, n, start, count)
            if k == 0:
                velocity_phase(old, new, props, *part)
            else:
                final = outs if t == lay.steps - 1 else None
                stress_phase(lay, old, new, props, push_in, t, *part, final)


def sees_all(n_we, width):
    return n_we <= 2 * width + 1 and n_we & (n_we - 1) == 0


def devices_in_view(n_we, width):
    return n_we if sees_all(n_we, width) else 2 * width + 1


def is_square(n_we, width):
    return sees_all(n_we, width) and n_we == 4


def shards(
    velocity, stress, memory, material_code, block_scale, material_table, source_cell, source_amp
):
    _, cx, cy, cz = velocity.shape
    sources, steps = source_amp.shape[2:]
    n_we, n_sn = lax.axis_size("we"), lax.axis_size("sn")
    reach = 3 * steps
    assert cz == LANES and cy >= reach and cx % BLK == 0 and cy % BLK == 0
    assert sources * (steps + 1) <= LANES

    used = FIELDS * cx * cy + (cx // BLK) * (cy // BLK) + 1
    vmem = pl.BlockSpec(memory_space=pltpu.VMEM)
    smem = pl.BlockSpec(memory_space=pltpu.SMEM)
    anywhere = pl.BlockSpec(memory_space=pl.ANY)

    def flat(x):
        return jnp.swapaxes(x, -3, -2).reshape(-1, LANES)

    assert material_table.shape[1] < LANES
    own, table = pl.pallas_call(
        functools.partial(pack_kernel, field=cx * cy),
        out_shape=[
            pltpu.VMEM((n, LANES), jnp.float32) for n in (round_up(used, SUB), SUB)
        ],
        in_specs=[anywhere, anywhere, anywhere, vmem, smem, smem, smem, smem],
        out_specs=[vmem, vmem],
        scratch_shapes=[pltpu.SemaphoreType.DMA((3,))],
        name="pack",
    )(
        flat(velocity),
        flat(stress),
        flat(memory),
        flat(material_code),
        jnp.swapaxes(block_scale, 0, 1),
        source_cell,
        source_amp,
        material_table,
    )

    width = -(-reach // cx)
    everything = sees_all(n_we, width)
    if everything:
        dests = list(range(n_we))
        window, fixed = n_we * cx, None
        moves = [[(i, i ^ k) for i in range(n_we)] for k in dests]
    else:
        dests = [0] + [sign * k for k in range(1, width + 1) for sign in (1, -1)]
        window, fixed = (2 * width + 1) * cx, width * cx
        moves = [[(i, i + k) for i in range(n_we) if 0 <= i + k < n_we] for k in dests]
    inner = [(i, i ^ 1) for i in range(n_sn) if i ^ 1 < n_sn]
    outer = [(i, i - 1 + 2 * (i % 2)) for i in range(n_sn)]
    outer = [(a, b) for a, b in outer if 0 <= b < n_sn]
    place = jnp.stack([lax.axis_index("we"), lax.axis_index("sn")])

    lay = Layout(cx, cy, steps, sources, window, dests, fixed)

    def frames(n, extra):
        return jax.ShapeDtypeStruct((n, window + extra, lay.rows, LANES), jnp.float32)

    early = min(EARLY_STEPS, steps - 1)
    state = [frames(6, 0), frames(steps, 0)]
    state += (early + 1) * [frames(3, 4), frames(6, 4), frames(6, 0)]
    params = pltpu.CompilerParams(vmem_limit_bytes=16 << 20)
    ready = {(0, CENTER, WHOLE): own}

    def send(block, axis, move, key):
        ready[key] = lax.ppermute(block, axis, move)

    last = len(dests) - 1
    assert last + 1 == devices_in_view(n_we, width)
    if is_square(n_we, width):
        half = SPLIT * cx * cy
        send(own, "we", moves[1], (1, CENTER, WHOLE))
        send(own, "we", moves[2], (2, CENTER, WHOLE))
        for i in range(3):
            block = ready[i, CENTER, WHOLE]
            send(block, "sn", outer, (i, OUTER, WHOLE))
            send(block, "sn", inner, (i, INNER, WHOLE))
        send(ready[1, CENTER, WHOLE][:half], "we", moves[2], (3, CENTER, FIRST))
        send(ready[2, CENTER, WHOLE][half:], "we", moves[1], (3, CENTER, SECOND))
        send(ready[3, CENTER, FIRST], "sn", outer, (3, OUTER, FIRST))
        send(ready[0, OUTER, WHOLE][half:], "we", moves[3], (3, OUTER, SECOND))
        send(ready[3, CENTER, FIRST], "sn", inner, (3, INNER, FIRST))
        send(ready[3, CENTER, SECOND], "sn", inner, (3, INNER, SECOND))
        plan = [
            [(0, CENTER, WHOLE)],
            [(k, CENTER, WHOLE) for k in (1, 2)] + [(0, INNER, WHOLE), (0, OUTER, WHOLE)],
            [(1, INNER, WHOLE), (1, OUTER, WHOLE)],
            [(3, CENTER, FIRST), (3, CENTER, SECOND), (2, INNER, WHOLE)]
            + [(3, INNER, FIRST), (3, INNER, SECOND)],
        ]
    else:
        plan = []
        for i, move in enumerate(moves):
            if i > 0:
                send(own, "we", move, (i, CENTER, WHOLE))
            block = ready[i, CENTER, WHOLE]
            send(block, "sn", outer, (i, OUTER, WHOLE))
            send(block, "sn", inner, (i, INNER, WHOLE))
            plan.append([(i, CENTER, WHOLE)])
            if i > 0:
                plan[i].append((i - 1, INNER, WHOLE))
            if i == last:
                plan[i].append((i, INNER, WHOLE))
            elif i > 0:
                plan[i].append((i - 1, OUTER, WHOLE))

    held = []
    for i, jobs in enumerate(plan):
        parts = [ready[job] for job in jobs]
        extra = len(parts) + 2
        held = pl.pallas_call(
            functools.partial(
                stage_kernel,
                lay=lay,
                jobs=jobs,
                initial=i == 0,
                final=i == len(plan) - 1,
                held=len(state),
            ),
            out_shape=state,
            in_specs=[vmem] * (extra - 1) + [smem] + [vmem] * len(held),
            out_specs=[vmem] * len(state),
            input_output_aliases={extra + k: k for k in range(len(held))},
            compiler_params=params,
        )(*parts, table, place, *held)
    done = [job for jobs in plan for job in jobs]
    jobs = [job for job in ready if job not in done]
    parts = [ready[job] for job in jobs]
    extra = len(parts) + 2
    results = [jax.ShapeDtypeStruct((n * cx * cy, LANES), jnp.float32) for n in (3, 6, 6)]
    outs = pl.pallas_call(
        functools.partial(late_kernel, lay=lay, jobs=jobs, held=len(state)),
        out_shape=results + state,
        in_specs=[vmem] * (extra - 1) + [smem] + [vmem] * len(state),
        out_specs=[vmem] * (3 + len(state)),
        input_output_aliases={extra + i: 3 + i for i in range(len(state))},
        compiler_params=params,
        name="late",
    )(*parts, table, place, *held)
    return tuple(jnp.swapaxes(x.reshape(-1, cy, cx, cz), 1, 2) for x in outs[:3])


def solution(mesh):
    in_specs = (
        P(None, "we", "sn", None),
        P(None, "we", "sn", None),
        P(None, "we", "sn", None),
        P("we", "sn", None),
        P("we", "sn", None),
        P(),
        P("we", "sn", None),
        P("we", "sn", None, None),
    )
    out_specs = (P(None, "we", "sn", None), P(None, "we", "sn", None), P(None, "we", "sn", None))

    def call(*args):
        step = jax.shard_map(
            shards, mesh=mesh, in_specs=in_specs, out_specs=out_specs, check_vma=False
        )
        return step(*args)

    return call
```

```python
import functools

import jax
import jax.numpy as jnp
from jax import lax
from jax.experimental import pallas as pl
from jax.experimental.pallas import tpu as pltpu
from jax.sharding import PartitionSpec as P


BLK = 4
BLKZ = 32
LANES = 128
SUB = 8

inner_coef = 9.0 / 8.0
outer_coef = 1.0 / 24.0
ratio = outer_coef / inner_coef
time_step = 0.08
friction = 0.4
half_step = 0.5 * time_step
largest = 3.0e38

VEL, STR, MEM, COD = 0, 3, 9, 15
FIELDS = 16
SPLIT = 8
WHOLE, FIRST, SECOND = 0, 1, 2
HELD = (range(FIELDS), range(SPLIT), range(SPLIT, FIELDS))
NORMAL = (0, 4, 5)
UNROLL = (16, 14)


def round_up(value, step):
    return -(-value // step) * step


def pack_kernel(*refs, field):
    vel, stress, mem = refs[:3]
    out, table = refs[8:10]
    near = refs[10:15]
    sem = refs[15]
    small = [
        pltpu.make_async_copy(far, to, sem.at[3 + i])
        for i, (far, to) in enumerate(zip(refs[3:8], near))
    ]
    for copy in small:
        copy.start()
    code, scale, cell, amp, kinds = near
    copies = []
    for i, (at, part) in enumerate(((VEL, vel), (STR, stress), (MEM, mem))):
        to = out.at[pl.ds(at * field, part.shape[0]), :]
        copies.append(pltpu.make_async_copy(part, to, sem.at[i]))
        copies[-1].start()
    for copy in small:
        copy.wait()
    out[COD * field : (COD + 1) * field, :] = (code[...] + 1).astype(jnp.float32)
    lane = lax.broadcasted_iota(jnp.int32, (1, LANES), 1)
    here = FIELDS * field
    for i in range(scale.shape[1]):
        for j in range(scale.shape[0]):
            row = jnp.zeros((1, LANES), jnp.float32)
            for k in range(scale.shape[2]):
                row = jnp.where(lane // BLKZ == k, scale[j, i, k], row)
            out[here : here + 1, :] = row
            here += 1
    size = out.shape[0]
    if here < size - 1:
        out[here : size - 1, :] = jnp.zeros((size - 1 - here, LANES), jnp.float32)
    count, steps = amp.shape[2], amp.shape[3]
    row = jnp.zeros((1, LANES), jnp.float32)
    for k in range(count):
        row = jnp.where(lane == k, cell[0, 0, k].astype(jnp.float32), row)
        for t in range(steps):
            row = jnp.where(lane == count + k * steps + t, time_step * amp[0, 0, k, t], row)
    out[size - 1 : size, :] = row
    per_step = time_step * inner_coef
    lines = [jnp.zeros((1, LANES), jnp.float32) for _ in range(table.shape[0])]
    for k in range(kinds.shape[1]):
        decay = kinds[3, k]
        values = (
            kinds[0, k] * per_step,
            kinds[1, k] * per_step,
            kinds[2, k] * per_step,
            decay,
            (1.0 - decay) * kinds[4, k] * (half_step / time_step),
            kinds[5, k],
        )
        for i, value in enumerate(values):
            lines[i] = jnp.where(lane == k + 1, value, lines[i])
    for i, line in enumerate(lines):
        table[i : i + 1, :] = line
    for copy in copies:
        copy.wait()


def divisor(n, top):
    return max(k for k in range(1, top + 1) if n % k == 0)


class Layout:
    def __init__(self, cx, cy, steps, sources, window, dests, fixed):
        self.cx, self.cy, self.steps, self.sources = cx, cy, steps, sources
        self.window, self.dests, self.fixed = window, tuple(dests), fixed
        self.field = cx * cy
        self.margin = 4
        low = self.margin + cy - 3 * steps + 1
        self.rows = round_up(low + round_up(cy + 6 * steps - 2, SUB) + 2, SUB)

    def base_plane(self, s, me):
        if self.fixed is None:
            return jnp.bitwise_xor(me, self.dests[s]) * self.cx
        return self.fixed - self.dests[s] * self.cx

    def tiles(self, reach):
        return self.margin + self.cy - reach, -(-(self.cy + 2 * reach) // SUB)

    def planes(self, reach, me):
        if self.fixed is not None:
            return self.fixed - reach, self.cx + 2 * reach
        own = [w * self.cx for w in range(self.window // self.cx)]
        need = max(
            min(w + self.cx + reach, self.window) - max(w - reach, 0) for w in own
        )
        need += need % 2 if need < self.window else 0
        return jnp.clip(me * self.cx - reach, 0, self.window - need), need


class State:
    def __init__(self, vel, stress, mem):
        self.vel, self.stress, self.mem = vel, stress, mem


def unpack(lay, block, part, table, state, props, push_in, plane, row, last_step):
    cx, cy, sources, steps = lay.cx, lay.cy, lay.sources, lay.steps
    shape = (cy, LANES)
    size = block.shape[0]

    held = HELD[part]

    def piece(f, p):
        return block[pl.ds((f - held.start) * lay.field + p, cy, stride=cx), :]

    def copy_fields(p):
        for c in range(3):
            if VEL + c in held:
                state.vel[c, plane + p + 2, pl.ds(row, cy), :] = piece(VEL + c, p)
        for c in range(6):
            if STR + c in held:
                state.stress[c, plane + p + 2, pl.ds(row, cy), :] = piece(STR + c, p)
            if MEM + c in held:
                state.mem[c, plane + p, pl.ds(row, cy), :] = piece(MEM + c, p) * half_step

    if COD not in held:
        for p in range(cx):
            copy_fields(p)
        return

    line = block[size - 1 : size, :]
    spot = [
        jnp.broadcast_to(line[:, k : k + 1], shape) for k in range(sources * (1 + steps))
    ]
    number = lax.broadcasted_iota(jnp.int32, shape, 0) * LANES
    number = (number + lax.broadcasted_iota(jnp.int32, shape, 1)).astype(jnp.float32)
    lines = [jnp.broadcast_to(table[k : k + 1, :], (SUB, LANES)) for k in range(6)]
    across = cy // BLK
    for i in range(cx // BLK):
        first = len(held) * lay.field + i * across
        grow = jnp.concatenate(
            [
                jnp.broadcast_to(block[first + j : first + j + 1, :], (BLK, LANES))
                for j in range(across)
            ],
            axis=0,
        )
        for p in range(i * BLK, (i + 1) * BLK):
            copy_fields(p)
            code = jnp.clip(piece(COD, p).astype(jnp.int32), 0, LANES - 1)
            for lo in range(0, cy, SUB):
                n = min(SUB, cy - lo)
                index = code[lo : lo + n]
                for k in range(6):
                    value = jnp.take_along_axis(lines[k][:n], index, axis=1)
                    if k in (1, 2):
                        value = value * grow[lo : lo + n]
                    props[k, plane + p, pl.ds(row + lo, n), :] = value
            hits = [spot[k] == number + float(p * cy * LANES) for k in range(sources)]
            for t in range(last_step):
                total = jnp.zeros(shape, jnp.float32)
                for k in range(sources):
                    total = total + jnp.where(hits[k], spot[sources + k * steps + t], 0.0)
                push_in[t, plane + p, pl.ds(row, cy), :] = total


def deep(f, k):
    lane = lax.broadcasted_iota(jnp.int32, f.shape, 1)
    moved = pltpu.roll(f, (-k) % LANES, 1)
    keep = lane < LANES - k if k > 0 else lane >= -k
    return jnp.where(keep, moved, 0.0)


def z_back(f):
    return f - deep(f, -1), deep(f, 1) - deep(f, -2)


def z_fore(f):
    return deep(f, 1) - f, deep(f, 2) - deep(f, -1)


def add(*pairs):
    one, two = pairs[0]
    for a, b in pairs[1:]:
        one = one + a
        two = two + b
    return one - ratio * two


class Reader:
    def __init__(self, ref, c, p, r):
        self.ref, self.c, self.p, self.r = ref, c, p, r

    def at(self, dp=0, dr=0):
        return self.ref[self.c, self.p + 2 + dp, pl.ds(self.r + dr, SUB), :]

    def x_fore(self):
        return self.at(1) - self.at(0), self.at(2) - self.at(-1)

    def x_back(self):
        return self.at(0) - self.at(-1), self.at(1) - self.at(-2)

    def y_fore(self):
        return self.at(0, 1) - self.at(0, 0), self.at(0, 2) - self.at(0, -1)

    def y_back(self):
        return self.at(0, 0) - self.at(0, -1), self.at(0, 1) - self.at(0, -2)


def velocity_phase(old, new, props, first, n, start, count):
    def body(i, carry):
        p = first + i
        for r in [start + SUB * j for j in range(count)]:
            sxx, sxz, sxy, syz, syy, szz = [Reader(old.stress, c, p, r) for c in range(6)]
            push = props[0, p, pl.ds(r, SUB), :]
            forces = (
                add(sxx.x_fore(), sxy.y_back(), z_back(sxz.at())),
                add(sxy.x_back(), syy.y_fore(), z_back(syz.at())),
                add(sxz.x_back(), syz.y_back(), z_fore(szz.at())),
            )
            for c in range(3):
                now = old.vel[c, p + 2, pl.ds(r, SUB), :]
                new.vel[c, p + 2, pl.ds(r, SUB), :] = now + push * forces[c]
        return carry

    lax.fori_loop(0, n, body, 0, unroll=divisor(n, UNROLL[0]))


def stress_phase(lay, old, new, props, push_in, t, first, n, start, count, outs=None):
    def body(i, carry):
        p = first + i
        for j in range(count):
            r = start + SUB * j
            here = pl.ds(r, SUB)
            ve, vn, vd = [Reader(new.vel, c, p, r) for c in range(3)]
            exx = add(ve.x_back())
            eyy = add(vn.y_back())
            ezz = add(z_back(vd.at()))
            exz = add(z_fore(ve.at()), vd.x_fore())
            exy = add(ve.y_fore(), vn.x_fore())
            eyz = add(z_fore(vn.at()), vd.y_fore())
            mu = props[2, p, here, :]
            twice = mu + mu
            bulk = props[1, p, here, :] * (exx + eyy + ezz)
            moves = (
                bulk + twice * exx,
                mu * exz,
                mu * exy,
                mu * eyz,
                bulk + twice * eyy,
                bulk + twice * ezz,
            )
            keep = props[3, p, here, :]
            gain = props[4, p, here, :]
            source = push_in[t, p, here, :]
            trial = []
            rest = []
            for c in range(6):
                before = old.mem[c, p, here, :]
                after = keep * before + gain * moves[c]
                rest.append(after)
                now = old.stress[c, p + 2, here, :]
                if c in NORMAL:
                    now = now + source
                trial.append((now + moves[c]) - (before + after))
            mean = (trial[0] + trial[4] + trial[5]) * (1.0 / 3.0)
            dxx, dyy, dzz = trial[0] - mean, trial[4] - mean, trial[5] - mean
            dxz, dxy, dyz = trial[1], trial[2], trial[3]
            second = 0.5 * (dxx * dxx + dyy * dyy + dzz * dzz) + (
                dxz * dxz + dxy * dxy + dyz * dyz
            )
            soft = jnp.maximum(-mean, 0.0) + jnp.log(1.0 + jnp.exp(-jnp.abs(mean)))
            level = props[5, p, here, :] + friction * soft
            scaled = second / (level * level)
            grown = jnp.minimum(1.0 + scaled * scaled, largest)
            factor = lax.rsqrt(grown * lax.rsqrt(grown))
            done = (
                mean + factor * dxx,
                factor * dxz,
                factor * dxy,
                factor * dyz,
                mean + factor * dyy,
                mean + factor * dzz,
            )
            if outs is not None:
                lo = SUB * j
                n_rows = min(SUB, lay.cy - lo)

                def put(out, c, value):
                    at = c * lay.field + lo * lay.cx + i
                    out[pl.ds(at, n_rows, stride=lay.cx), :] = value[:n_rows]

                for c, part in enumerate((ve, vn, vd)):
                    put(outs[0], c, part.at())
                for c in range(6):
                    put(outs[1], c, done[c])
                    put(outs[2], c, rest[c] * (1.0 / half_step))
            else:
                for c in range(6):
                    new.stress[c, p + 2, here, :] = done[c]
                    new.mem[c, p, here, :] = rest[c]
        return carry

    lax.fori_loop(0, n, body, 0, unroll=divisor(n, UNROLL[1]))


CENTER, INNER, OUTER = 0, 1, 2
EARLY_STEPS = 2


def unpack_jobs(lay, blocks, jobs, table, state, props, push_in, me, odd):
    cy, margin, steps = lay.cy, lay.margin, lay.steps
    rows = (
        margin + cy,
        jnp.where(odd == 0, margin + 2 * cy, margin),
        jnp.where(odd == 0, margin, margin + 2 * cy),
    )
    for block, (s, kind, part) in zip(blocks, jobs):
        plane = lay.base_plane(s, me)
        pushes = steps if kind == CENTER else steps - 1
        unpack(lay, block, part, table, state, props, push_in, plane, rows[kind], pushes)


def states_of(refs):
    return [State(*refs[i : i + 3]) for i in range(0, len(refs), 3)]


def stage_kernel(*refs, lay, jobs, initial, final, held):
    blocks = refs[: len(jobs)]
    table, place = refs[len(jobs) : len(jobs) + 2]
    refs = refs[-held:]
    props, push_in = refs[:2]
    states = states_of(refs[2:])
    me, odd = place[0], lax.rem(place[1], 2)

    if initial:
        blank = jnp.zeros((lay.rows, LANES), jnp.float32)
        for p in (0, 1, lay.window + 2, lay.window + 3):
            for c in range(3):
                for i, state in enumerate(states):
                    if i > 0:
                        state.vel[c, p] = blank
                    state.stress[c, p] = blank
    unpack_jobs(lay, blocks, jobs, table, states[0], props, push_in, me, odd)
    if not final:
        return

    for t in range(len(states) - 1):
        for k in (0, 1):
            reach, late = split(lay, t, k)
            start, count = lay.tiles(reach)
            first, n = lay.planes(reach, me)
            end = start + lay.cy + 2 * reach
            at = jnp.where(odd == 0, end - SUB * (count - late), start)
            part = (first, n, at, count - late)
            if k == 0:
                velocity_phase(states[t], states[t + 1], props, *part)
            else:
                stress_phase(lay, states[t], states[t + 1], props, push_in, t, *part)


def split(lay, t, k):
    reach = 3 * (lay.steps - 1 - t) + (2 if k == 0 else 0)
    return reach, -(-(reach + 4 * t + 2 * k + 2) // SUB)


def late_kernel(*refs, lay, jobs, held):
    count = len(jobs)
    blocks = refs[:count]
    table, place = refs[count : count + 2]
    outs = refs[count + 2 + held : count + 5 + held]
    refs = refs[-held:]
    props, push_in = refs[:2]
    states = states_of(refs[2:])
    me, odd = place[0], lax.rem(place[1], 2)
    unpack_jobs(lay, blocks, jobs, table, states[0], props, push_in, me, odd)

    for t in range(lay.steps):
        for k in (0, 1):
            reach, late = split(lay, t, k)
            start, count = lay.tiles(reach)
            first, n = lay.planes(reach, me)
            if t + 1 < len(states):
                old, new = states[t], states[t + 1]
                end = start + lay.cy + 2 * reach
                part = (first, n, jnp.where(odd == 0, start, end - SUB * late), late)
            else:
                old = new = states[-1]
                part = (first, n, start, count)
            if k == 0:
                velocity_phase(old, new, props, *part)
            else:
                final = outs if t == lay.steps - 1 else None
                stress_phase(lay, old, new, props, push_in, t, *part, final)


def sees_all(n_we, width):
    return n_we <= 2 * width + 1 and n_we & (n_we - 1) == 0


def devices_in_view(n_we, width):
    return n_we if sees_all(n_we, width) else 2 * width + 1


def is_square(n_we, width):
    return sees_all(n_we, width) and n_we == 4


def shards(
    velocity, stress, memory, material_code, block_scale, material_table, source_cell, source_amp
):
    _, cx, cy, cz = velocity.shape
    sources, steps = source_amp.shape[2:]
    n_we, n_sn = lax.axis_size("we"), lax.axis_size("sn")
    reach = 3 * steps
    assert cz == LANES and cy >= reach and cx % BLK == 0 and cy % BLK == 0
    assert sources * (steps + 1) <= LANES

    used = FIELDS * cx * cy + (cx // BLK) * (cy // BLK) + 1
    vmem = pl.BlockSpec(memory_space=pltpu.VMEM)
    smem = pl.BlockSpec(memory_space=pltpu.SMEM)
    anywhere = pl.BlockSpec(memory_space=pl.ANY)

    def flat(x):
        return jnp.swapaxes(x, -3, -2).reshape(-1, LANES)

    assert material_table.shape[1] < LANES
    small = (jnp.swapaxes(block_scale, 0, 1), source_cell, source_amp, material_table)
    own, table = pl.pallas_call(
        functools.partial(pack_kernel, field=cx * cy),
        out_shape=[
            pltpu.VMEM((n, LANES), jnp.float32) for n in (round_up(used, SUB), SUB)
        ],
        in_specs=[anywhere] * 8,
        out_specs=[vmem, vmem],
        scratch_shapes=[pltpu.VMEM((cx * cy, LANES), jnp.int32)]
        + [pltpu.SMEM(x.shape, x.dtype) for x in small]
        + [pltpu.SemaphoreType.DMA((8,))],
        name="pack",
    )(
        flat(velocity),
        flat(stress),
        flat(memory),
        flat(material_code),
        *small,
    )

    width = -(-reach // cx)
    everything = sees_all(n_we, width)
    if everything:
        dests = list(range(n_we))
        window, fixed = n_we * cx, None
        moves = [[(i, i ^ k) for i in range(n_we)] for k in dests]
    else:
        dests = [0] + [sign * k for k in range(1, width + 1) for sign in (1, -1)]
        window, fixed = (2 * width + 1) * cx, width * cx
        moves = [[(i, i + k) for i in range(n_we) if 0 <= i + k < n_we] for k in dests]
    inner = [(i, i ^ 1) for i in range(n_sn) if i ^ 1 < n_sn]
    outer = [(i, i - 1 + 2 * (i % 2)) for i in range(n_sn)]
    outer = [(a, b) for a, b in outer if 0 <= b < n_sn]
    place = jnp.stack([lax.axis_index("we"), lax.axis_index("sn")])

    lay = Layout(cx, cy, steps, sources, window, dests, fixed)

    def frames(n, extra):
        return jax.ShapeDtypeStruct((n, window + extra, lay.rows, LANES), jnp.float32)

    early = min(EARLY_STEPS, steps - 1)
    state = [frames(6, 0), frames(steps, 0)]
    state += (early + 1) * [frames(3, 4), frames(6, 4), frames(6, 0)]
    params = pltpu.CompilerParams(vmem_limit_bytes=16 << 20)
    ready = {(0, CENTER, WHOLE): own}

    def send(block, axis, move, key):
        ready[key] = lax.ppermute(block, axis, move)

    last = len(dests) - 1
    assert last + 1 == devices_in_view(n_we, width)
    if is_square(n_we, width):
        half = SPLIT * cx * cy
        send(own, "we", moves[1], (1, CENTER, WHOLE))
        send(own, "we", moves[2], (2, CENTER, WHOLE))
        for i in range(3):
            block = ready[i, CENTER, WHOLE]
            send(block, "sn", outer, (i, OUTER, WHOLE))
            send(block, "sn", inner, (i, INNER, WHOLE))
        send(ready[1, CENTER, WHOLE][:half], "we", moves[2], (3, CENTER, FIRST))
        send(ready[2, CENTER, WHOLE][half:], "we", moves[1], (3, CENTER, SECOND))
        send(ready[3, CENTER, FIRST], "sn", outer, (3, OUTER, FIRST))
        send(ready[0, OUTER, WHOLE][half:], "we", moves[3], (3, OUTER, SECOND))
        send(ready[3, CENTER, FIRST], "sn", inner, (3, INNER, FIRST))
        send(ready[3, CENTER, SECOND], "sn", inner, (3, INNER, SECOND))
        plan = [
            [(0, CENTER, WHOLE)],
            [(k, CENTER, WHOLE) for k in (1, 2)] + [(0, INNER, WHOLE), (0, OUTER, WHOLE)],
            [(1, INNER, WHOLE), (1, OUTER, WHOLE)],
            [(3, CENTER, FIRST), (3, CENTER, SECOND), (2, INNER, WHOLE)]
            + [(3, INNER, FIRST), (3, INNER, SECOND), (2, OUTER, WHOLE)],
        ]
    else:
        plan = []
        for i, move in enumerate(moves):
            if i > 0:
                send(own, "we", move, (i, CENTER, WHOLE))
            block = ready[i, CENTER, WHOLE]
            send(block, "sn", outer, (i, OUTER, WHOLE))
            send(block, "sn", inner, (i, INNER, WHOLE))
            plan.append([(i, CENTER, WHOLE)])
            if i > 0:
                plan[i].append((i - 1, INNER, WHOLE))
            if i == last:
                plan[i].append((i, INNER, WHOLE))
            elif i > 0:
                plan[i].append((i - 1, OUTER, WHOLE))

    held = []
    for i, jobs in enumerate(plan):
        parts = [ready[job] for job in jobs]
        extra = len(parts) + 2
        held = pl.pallas_call(
            functools.partial(
                stage_kernel,
                lay=lay,
                jobs=jobs,
                initial=i == 0,
                final=i == len(plan) - 1,
                held=len(state),
            ),
            out_shape=state,
            in_specs=[vmem] * (extra - 1) + [smem] + [vmem] * len(held),
            out_specs=[vmem] * len(state),
            input_output_aliases={extra + k: k for k in range(len(held))},
            compiler_params=params,
        )(*parts, table, place, *held)
    done = [job for jobs in plan for job in jobs]
    jobs = [job for job in ready if job not in done]
    parts = [ready[job] for job in jobs]
    extra = len(parts) + 2
    results = [jax.ShapeDtypeStruct((n * cx * cy, LANES), jnp.float32) for n in (3, 6, 6)]
    outs = pl.pallas_call(
        functools.partial(late_kernel, lay=lay, jobs=jobs, held=len(state)),
        out_shape=results + state,
        in_specs=[vmem] * (extra - 1) + [smem] + [vmem] * len(state),
        out_specs=[vmem] * (3 + len(state)),
        input_output_aliases={extra + i: 3 + i for i in range(len(state))},
        compiler_params=params,
        name="late",
    )(*parts, table, place, *held)
    return tuple(jnp.swapaxes(x.reshape(-1, cy, cx, cz), 1, 2) for x in outs[:3])


def solution(mesh):
    in_specs = (
        P(None, "we", "sn", None),
        P(None, "we", "sn", None),
        P(None, "we", "sn", None),
        P("we", "sn", None),
        P("we", "sn", None),
        P(),
        P("we", "sn", None),
        P("we", "sn", None, None),
    )
    out_specs = (P(None, "we", "sn", None), P(None, "we", "sn", None), P(None, "we", "sn", None))

    def call(*args):
        step = jax.shard_map(
            shards, mesh=mesh, in_specs=in_specs, out_specs=out_specs, check_vma=False
        )
        return step(*args)

    return call
```
